256 devices in a mesh: gx: 16 (over y_lo, z), gy: 16 (over x, y_hi, core).
Axes of the slice: x: 4, y: 4 (y_hi: 2, y_lo: 2; y = y_hi * 2 + y_lo), z: 8, core: 2. Of those that a mesh axis runs over, the one named last changes fastest.
Arguments:
- adjoint: float32 [4, 256, 512, 128], P(None, 'gx', 'gy'), may hold values from -6 to 6
- velocity: bfloat16 [3, 256, 512, 128], P(None, 'gx', 'gy'), may hold values from -3 to 3
- diffusivity: bfloat16 [256, 512, 128], P('gx', 'gy'), may hold values from 0.049804688 to 0.796875
- concentration: bfloat16 [256, 512, 128], P('gx', 'gy'), may hold values from -4 to 4
- heights: int32 [256, 512], P('gx', 'gy'), may hold values from 0 to 32
- receptors: int32 [16, 16, 64], P('gx', 'gy'), may hold values from 0 to 65535
- face_src: int32 [16, 16, 16, 16], P('gx', 'gy'), may hold values from -1 to 511, as said below
- face_dst: int32 [16, 16, 16, 16], P('gx', 'gy'), may hold values from 0 to 511
- face_coef: float32 [16, 16, 16, 16, 128], P('gx', 'gy'), may hold values from 0.2 to 1
Outputs:
- adjoint_out: float32 [4, 256, 512, 128], P(None, 'gx', 'gy')
The draws below stay inside these ranges and needn't reach their ends.
Inputs may be any that keep to these rules, and one draw needn't show every extreme that they name: `face_src`: -1 marks an empty slot; the slots of one source tile and owner are filled from the front; at most 16 live slots for one source and owner, reached for some owner of every source tile and for one owner from every source.
All inputs are finite; a program needn't handle non-finite values.
Results may differ from the reference program's by a relative error of at most 0.0003.
Values may be sent and summed in bfloat16 or wider, within the bound.
No kernel may reach another device: no remote copies, remote signals or barrier semaphores. Data moves between devices by JAX's collectives and lax.ppermute only.
A program may use at most 64 MiB of HBM per device.

```python
import math
import jax
import jax.numpy as jnp

CX = 16
CY = 32
CZ = 128
CAP = 16
RCP = 64
HMAX = 32
STEPS = 2
TILES_X = 16
TILES_Y = 16
NX = 256
NY = 512


def draw_face_src(key, part):
    key_count, key_busy, key_owner, key_cols = jax.random.split(key, 4)
    counts = jax.random.randint(key_count, (TILES_X, TILES_Y, TILES_X), CAP // 4, CAP + 1)
    busy = jax.random.randint(key_busy, (TILES_X, TILES_Y, 1), 0, TILES_X)
    full_owner = jax.random.randint(key_owner, (), 0, TILES_X)
    owners = jnp.arange(TILES_X)[None, None, :]
    counts = jnp.where((owners == busy) | (owners == full_owner), CAP, counts)
    columns = jax.random.randint(key_cols, (TILES_X, TILES_Y, TILES_X, CAP), 0, CX * CY)
    slots = jnp.arange(CAP)
    return jnp.where(slots < counts[..., None], columns, -1).astype(jnp.int32)


def touch_ends(drawn, stream_key, low, top_value):
    spot = [jax.random.randint(jax.random.fold_in(stream_key, axis), (), 0, length) for axis, length in enumerate(drawn.shape)]
    longest = drawn.shape.index(max(drawn.shape))
    neighbour = spot[:longest] + [(spot[longest] + 1) % drawn.shape[longest]] + spot[longest + 1:]
    return drawn.at[tuple(spot)].set(low).at[tuple(neighbour)].set(top_value)


def shard_levels(rng, shape, cuts, least, high):
    factor_of = 1.0
    for dim, shards_of in cuts:
        draws = jax.random.uniform(jax.random.fold_in(jax.random.fold_in(rng, 6), dim), (shards_of,), jnp.float32, least / len(cuts), high / len(cuts))
        factor_of = factor_of * jnp.repeat(jnp.exp(draws), shape[dim] // shards_of).reshape((-1,) + (1,) * (len(shape) - 1 - dim))
    return factor_of


def gaussian(own_key, shape, scale, most, cuts=(), held_as=jnp.bfloat16):
    result = scale * jax.random.normal(own_key, shape, jnp.float32)
    if cuts:
        result = result * shard_levels(own_key, shape, cuts, -0.22, 0.18)
    return jnp.clip(result, -most, most).astype(held_as)


def setup_inputs(seed: int = 0) -> dict:
    keys = jax.random.split(jax.random.key(seed), 10)
    adjoint = gaussian(keys[0], (4, NX, NY, CZ), 1.0, 6.0, ((1, 16), (2, 16)), jnp.float32)
    velocity = gaussian(keys[1], (3, NX, NY, CZ), 1.0, 3.0, ((1, 16), (2, 16)))
    diffusivity = jnp.clip(jnp.exp(math.log(0.796875) - 2.7725887 * jax.random.uniform(keys[2], (NX, NY, CZ), jnp.float32) ** shard_levels(keys[2], (NX, NY, CZ), ((0, 16), (1, 16)), -0.2, 0.2)), 0.049804688, 0.796875).astype(jnp.bfloat16)
    concentration = gaussian(keys[3], (NX, NY, CZ), 1.0, 4.0, ((0, 16), (1, 16)))
    heights = touch_ends(jax.random.randint(keys[4], (NX, NY), 0, HMAX + 1), jax.random.fold_in(keys[4], 1), 0, HMAX).astype(jnp.int32)
    receptors = touch_ends(jax.random.randint(keys[5], (TILES_X, TILES_Y, RCP), 0, CX * CY * CZ), jax.random.fold_in(keys[5], 1), 0, (CX * CY * CZ) - 1).astype(jnp.int32)
    face_src = draw_face_src(jax.random.fold_in(keys[9], 71), 0)
    face_dst = touch_ends(jax.random.randint(keys[7], (TILES_X, TILES_Y, TILES_X, CAP), 0, CX * CY), jax.random.fold_in(keys[7], 1), 0, (CX * CY) - 1).astype(jnp.int32)
    face_coef = jnp.clip(0.2 + 0.8 * jax.random.uniform(keys[8], (TILES_X, TILES_Y, TILES_X, CAP, CZ), jnp.float32) ** shard_levels(keys[8], (TILES_X, TILES_Y, TILES_X, CAP, CZ), ((0, 16), (1, 16)), -0.2, 0.2), 0.2, 1.0)
    return dict(adjoint=adjoint, velocity=velocity, diffusivity=diffusivity, concentration=concentration, heights=heights, receptors=receptors, face_src=face_src, face_dst=face_dst, face_coef=face_coef)


TIME_STEP = 0.1


def shift_up(field):
    return jnp.concatenate([field[..., 1:], jnp.zeros_like(field[..., :1])], axis=-1)


def shift_down(field):
    return jnp.concatenate([jnp.zeros_like(field[..., :1]), field[..., :-1]], axis=-1)


def field_operator(padded, vel_pad, diff_pad):
    center = padded[..., 1:-1, 1:-1, :]
    k_center = diff_pad[1:-1, 1:-1]
    flux = vel_pad[0] * padded
    transport = flux[..., 2:, 1:-1, :] - flux[..., :-2, 1:-1, :]
    flux = vel_pad[1] * padded
    transport = transport + flux[..., 1:-1, 2:, :] - flux[..., 1:-1, :-2, :]
    flux = vel_pad[2, 1:-1, 1:-1] * center
    transport = transport + shift_up(flux) - shift_down(flux)
    spread = (k_center + diff_pad[2:, 1:-1]) * (padded[..., 2:, 1:-1, :] - center) - (k_center + diff_pad[:-2, 1:-1]) * (center - padded[..., :-2, 1:-1, :])
    spread = spread + (k_center + diff_pad[1:-1, 2:]) * (padded[..., 1:-1, 2:, :] - center) - (k_center + diff_pad[1:-1, :-2]) * (center - padded[..., 1:-1, :-2, :])
    spread = spread + (k_center + shift_up(k_center)) * (shift_up(center) - center) - (k_center + shift_down(k_center)) * (center - shift_down(center))
    return 0.5 * (transport + spread)


def gradient_part(conc_pad, component):
    if component == 0:
        return 0.5 * (conc_pad[2:, 1:-1] - conc_pad[:-2, 1:-1])
    if component == 1:
        return 0.5 * (conc_pad[1:-1, 2:] - conc_pad[1:-1, :-2])
    center = conc_pad[1:-1, 1:-1]
    return 0.5 * (shift_up(center) - shift_down(center))


def pad_sides(field):
    widths = [(0, 0)] * (field.ndim - 3) + [(1, 1), (1, 1), (0, 0)]
    return jnp.pad(field, widths)


def reference(adjoint, velocity, diffusivity, concentration, heights, receptors, face_src, face_dst, face_coef):
    vel_pad = pad_sides(velocity.astype(jnp.float32))
    diff_pad = pad_sides(diffusivity.astype(jnp.float32))
    conc_pad = pad_sides(concentration.astype(jnp.float32))
    levels = jnp.arange(CZ, dtype=jnp.int32)
    fluid = (levels[None, None, :] >= heights[:, :, None]).astype(jnp.float32)
    tile_x = jnp.arange(TILES_X, dtype=jnp.int32)[:, None, None]
    tile_y = jnp.arange(TILES_Y, dtype=jnp.int32)[None, :, None]
    rec_x = tile_x * CX + receptors // (CY * CZ)
    rec_y = tile_y * CY + (receptors // CZ) % CY
    rec_z = receptors % CZ
    live_slots = face_src >= 0
    src_cols = jnp.maximum(face_src, 0)
    source_x = jnp.arange(TILES_X, dtype=jnp.int32)[:, None, None, None]
    source_y = jnp.arange(TILES_Y, dtype=jnp.int32)[None, :, None, None]
    owner_x = jnp.arange(TILES_X, dtype=jnp.int32)[None, None, :, None]
    src_x = source_x * CX + src_cols // CY
    src_y = source_y * CY + src_cols % CY
    dst_cols = jnp.transpose(face_dst, (2, 1, 0, 3))
    dst_x = owner_x * CX + dst_cols // CY
    dst_y = source_y * CY + dst_cols % CY
    for step in range(STEPS):
        conc_adj = adjoint[3].at[rec_x, rec_y, rec_z].add(1.0)
        blocks = jnp.where(live_slots[..., None], face_coef * conc_adj[src_x, src_y], 0.0)
        wall_sum = jnp.zeros((NX, NY, CZ), jnp.float32).at[dst_x, dst_y].add(blocks)
        fields = []
        for component in range(4):
            field = conc_adj if component == 3 else adjoint[component]
            change = field_operator(pad_sides(field), vel_pad, diff_pad)
            if component < 3:
                change = change - conc_adj * gradient_part(conc_pad, component)
            updated = fluid * (field + TIME_STEP * change)
            if component == 2:
                updated = updated + wall_sum
            fields.append(updated)
        adjoint = jnp.stack(fields)
    return adjoint
```

```python
import jax
import jax.numpy as jnp
from jax import lax
from jax.experimental import pallas as pl
from jax.experimental.pallas import tpu as pltpu
from jax.sharding import PartitionSpec as P

F32 = jnp.float32
BF16 = jnp.bfloat16
PADY = 8
VMEM = pl.BlockSpec(memory_space=pltpu.VMEM)
HBM = pl.BlockSpec(memory_space=pltpu.HBM)


def split3(x):
    hi = x.astype(BF16)
    rest = x - hi.astype(F32)
    mid = rest.astype(BF16)
    low = (rest - mid.astype(F32)).astype(BF16)
    return jnp.concatenate([hi, mid, low], axis=1)


def join3(x):
    return x[:, :128] + x[:, 128:256] + x[:, 256:384]


def row_values(table):
    n = table.shape[1]
    eye = lax.broadcasted_iota(jnp.int32, (n, n), 0) == lax.broadcasted_iota(jnp.int32, (n, n), 1)
    high = table >> 4
    low = table & 15
    ones = jnp.ones((n, 128), BF16)
    total = None
    for part in (high * 16, low):
        part = part.astype(F32)
        rows = [
            jnp.where(eye, jnp.broadcast_to(part[d : d + 1], (n, n)), 0.0)
            for d in range(table.shape[0])
        ]
        spread = jnp.concatenate(rows, axis=0).astype(BF16)
        value = jnp.dot(spread, ones, preferred_element_type=F32)
        total = value if total is None else total + value
    return total


def select_rows(table, cols):
    index = row_values(table).astype(jnp.int32)
    lane = lax.broadcasted_iota(jnp.int32, index.shape, 1)
    hot = [(index == lane + t).astype(F32).astype(BF16) for t in range(0, cols, 128)]
    return jnp.concatenate(hot, axis=1)


def select_cols(table, cols):
    d_count, n = table.shape
    slots = d_count * n
    tile = (
        lax.broadcasted_iota(jnp.int32, (n, slots), 1) % n
        == lax.broadcasted_iota(jnp.int32, (n, slots), 0)
    ).astype(F32).astype(BF16)
    mine = (
        lax.broadcasted_iota(jnp.int32, (d_count, slots), 1) // n
        == lax.broadcasted_iota(jnp.int32, (d_count, slots), 0)
    )
    high = ((table >> 4) * 16).astype(F32).astype(BF16)
    low = (table & 15).astype(F32).astype(BF16)
    value = jnp.dot(high, tile, preferred_element_type=F32) + jnp.dot(
        low, tile, preferred_element_type=F32
    )
    line = jnp.sum(jnp.where(mine, value, 0.0), axis=0, keepdims=True).astype(jnp.int32)
    col = lax.broadcasted_iota(jnp.int32, (cols, slots), 0)
    return (col == line).astype(F32).astype(BF16)


def scatter_blocks(table, blocks, cols):
    hot = select_cols(table, cols)
    return join3(jnp.dot(hot, split3(blocks), preferred_element_type=F32))


def receptor_counts(line, cols):
    entries = line.shape[1]
    col = lax.broadcasted_iota(jnp.int32, (cols, entries), 0)
    level = lax.broadcasted_iota(jnp.int32, (128, entries), 0)
    hot_col = (col == (line >> 7)).astype(F32).astype(BF16)
    hot_level = (level == (line & 127)).astype(F32).astype(BF16)
    return lax.dot_general(
        hot_col, hot_level, (((1,), (1,)), ((), ())), preferred_element_type=F32
    )


def make_kernels(nx, ny, cx, cy, owners, cap):
    cols = cx * cy
    slots = owners * cap
    px, py = cx + 2, cy + 2 * PADY
    inside = (pl.ds(1, cx), pl.ds(PADY, cy))

    def edges_at():
        par_x = lax.rem(lax.axis_index("gx"), 2)
        par_y = lax.rem(lax.axis_index("gy"), 2)
        return (
            (cx - 1) * (1 - par_x), (cx - 1) * par_x,
            (cy - 1) * (1 - par_y), (cy - 1) * par_y,
        )

    def start_all(copies):
        for copy in copies:
            copy.start()

    def wait_all(copies):
        for copy in copies:
            copy.wait()

    def clear_halo(pad_ref, planes):
        zero = jnp.zeros((px, PADY, 128), F32)
        row = jnp.zeros((cy, 128), F32)
        for k in planes:
            pad_ref[k, :, 0:PADY, :] = zero
            pad_ref[k, :, PADY + cy : py, :] = zero
            pad_ref[k, 0, PADY : PADY + cy, :] = row
            pad_ref[k, cx + 1, PADY : PADY + cy, :] = row

    def take_halo(pad_ref, plane, n, xe_ref, xo_ref, ye_ref, yo_ref, with_x, with_y):
        me_x, me_y = lax.axis_index("gx"), lax.axis_index("gy")
        par_x, par_y = lax.rem(me_x, 2), lax.rem(me_y, 2)
        if with_x:
            e, o = xe_ref[n], xo_ref[n]
            before = jnp.where(par_x == 0, o, e)
            after = jnp.where(par_x == 0, e, o)
            pad_ref[plane, 0, PADY : PADY + cy, :] = jnp.where(me_x == 0, 0.0, before)
            pad_ref[plane, cx + 1, PADY : PADY + cy, :] = jnp.where(me_x == nx - 1, 0.0, after)
        if with_y:
            e, o = ye_ref[n], yo_ref[n]
            before = jnp.where(me_y == 0, 0.0, jnp.where(par_y == 0, o, e))
            after = jnp.where(me_y == ny - 1, 0.0, jnp.where(par_y == 0, e, o))
            for i in range(cx):
                pad_ref[plane, i + 1, PADY - 1 : PADY, :] = before[i : i + 1]
                pad_ref[plane, i + 1, PADY + cy : PADY + cy + 1, :] = after[i : i + 1]

    def fill_pads(pad_ref, vel_ref, dif_ref, con_ref):
        pad_ref[0, 1 : cx + 1, PADY : PADY + cy, :] = vel_ref[0].astype(F32)
        pad_ref[1, 1 : cx + 1, PADY : PADY + cy, :] = vel_ref[1].astype(F32)
        pad_ref[2, 1 : cx + 1, PADY : PADY + cy, :] = dif_ref[...].astype(F32)
        pad_ref[3, 1 : cx + 1, PADY : PADY + cy, :] = con_ref[...].astype(F32)

    def coefficients(pad_ref, vel_ref, fluid_ref, coef_ref):
        lane = lax.broadcasted_iota(jnp.int32, (8, 128), 1)
        level = lane.astype(F32)
        top = lane == 127
        bottom = lane == 0

        def up(x):
            return jnp.where(top, 0.0, pltpu.roll(x, 127, axis=1))

        def down(x):
            return jnp.where(bottom, 0.0, pltpu.roll(x, 1, axis=1))

        def body(i, carry):
            for half in range(cy // 16):
                uz2 = vel_ref[2, i, 16 * half : 16 * half + 16, :].astype(F32)
                for sub in range(2):
                    jv = 2 * half + sub
                    j = PADY + 8 * jv
                    lo = 8 * jv
                    at = pl.ds(pl.multiple_of(i * cy + lo, 8), 8)
                    uz = uz2[8 * sub : 8 * sub + 8]
                    fluid = (level >= fluid_ref[at, :]).astype(F32)
                    e = 0.05 * fluid
                    fluid_ref[at, :] = e
                    k0 = pad_ref[2, i + 1, j : j + 8, :]
                    ends = None
                    n = 1
                    for plane, plus, minus in (
                        (0, (i + 2, j), (i, j)),
                        (1, (i + 1, j + 1), (i + 1, j - 1)),
                    ):
                        for sign, (a, b) in ((1.0, plus), (-1.0, minus)):
                            kn = k0 + pad_ref[2, a, b : b + 8, :]
                            un = pad_ref[plane, a, b : b + 8, :]
                            coef_ref[n, at, :] = e * (kn + un if sign > 0 else kn - un)
                            ends = kn if ends is None else ends + kn
                            n += 1
                        coef_ref[7 + plane, at, :] = e * (
                            pad_ref[3, plus[0], plus[1] : plus[1] + 8, :]
                            - pad_ref[3, minus[0], minus[1] : minus[1] + 8, :]
                        )
                    kn = k0 + up(k0)
                    ends = ends + kn
                    coef_ref[5, at, :] = jnp.where(top, 0.0, e * (kn + up(uz)))
                    kn = k0 + down(k0)
                    ends = ends + kn
                    coef_ref[6, at, :] = jnp.where(bottom, 0.0, e * (kn - down(uz)))
                    c0 = pad_ref[3, i + 1, j : j + 8, :]
                    coef_ref[9, at, :] = e * (up(c0) - down(c0))
                    coef_ref[0, at, :] = fluid - e * ends
            return carry

        lax.fori_loop(0, cx, body, 0)

    def stencil(state_ref, coef_ref, extra, next_ref):
        def body(i, carry):
            for jv in range(cy // 8):
                j = PADY + 8 * jv
                at = pl.ds(pl.multiple_of(i * cy + 8 * jv, 8), 8)
                c = [coef_ref[n, at, :] for n in range(10)]
                conc = None
                for k in (3, 0, 1, 2):
                    f = state_ref[k, i + 1, j : j + 8, :]
                    if k == 3:
                        conc = f
                    value = c[0] * f
                    value = value + c[1] * state_ref[k, i + 2, j : j + 8, :]
                    value = value + c[2] * state_ref[k, i, j : j + 8, :]
                    value = value + c[3] * state_ref[k, i + 1, j + 1 : j + 9, :]
                    value = value + c[4] * state_ref[k, i + 1, j - 1 : j + 7, :]
                    value = value + c[5] * pltpu.roll(f, 127, axis=1)
                    value = value + c[6] * pltpu.roll(f, 1, axis=1)
                    if k < 3:
                        value = value - c[7 + k] * conc
                    for component, ref in extra:
                        if component == k:
                            value = value + ref[at, :]
                    next_ref[k, at, :] = value
            return carry

        lax.fori_loop(0, cx, body, 0)

    def edge_row(ref, k, row):
        return ref[k, pl.ds(pl.multiple_of(row * cy, 8), cy), :]

    def edge_col(ref, k, col):
        return ref[k, pl.ds(col, cx, stride=cy), :]

    def first(
        adj_hbm, vel_hbm, dif_hbm, con_hbm, rec_hbm, src_hbm, weight_hbm,
        blocks_ref, xe_ref, xo_ref, ye_ref, yo_ref,
        adj_ref, vel_ref, dif_ref, con_ref, rec_ref, src_ref, weight_ref, side_ref, sem,
    ):
        copies = [
            pltpu.make_async_copy(rec_hbm, rec_ref, sem.at[0]),
            pltpu.make_async_copy(adj_hbm.at[3], adj_ref.at[3], sem.at[1]),
            pltpu.make_async_copy(src_hbm, src_ref, sem.at[2]),
            pltpu.make_async_copy(weight_hbm, weight_ref, sem.at[3]),
            pltpu.make_async_copy(vel_hbm.at[pl.ds(0, 2)], vel_ref, sem.at[4]),
            pltpu.make_async_copy(dif_hbm, dif_ref, sem.at[5]),
            pltpu.make_async_copy(con_hbm, con_ref, sem.at[6]),
            pltpu.make_async_copy(adj_hbm.at[pl.ds(0, 3)], adj_ref.at[pl.ds(0, 3)], sem.at[7]),
        ]
        start_all(copies)
        row_e, row_o, col_e, col_o = edges_at()
        copies[0].wait()
        counts = receptor_counts(rec_ref[...], cols)
        copies[2].wait()
        hot = select_rows(src_ref[...], cols)
        copies[1].wait()
        conc = adj_ref[3] + counts
        adj_ref[3] = conc
        picked = join3(jnp.dot(hot, split3(conc), preferred_element_type=F32))
        copies[3].wait()
        blocks_ref[...] = weight_ref[...] * picked
        wait_all(copies[4:7])
        side_ref[0] = vel_ref[1].astype(F32).reshape(cols, 128)
        side_ref[1] = dif_ref[...].astype(F32).reshape(cols, 128)
        side_ref[2] = con_ref[...].astype(F32).reshape(cols, 128)
        for row, out in ((row_e, xe_ref), (row_o, xo_ref)):
            out[4] = vel_ref[0, row].astype(F32)
            out[5] = dif_ref[row].astype(F32)
            out[6] = con_ref[row].astype(F32)
        for col, out in ((col_e, ye_ref), (col_o, yo_ref)):
            for k in range(3):
                out[4 + k] = edge_col(side_ref, k, col)
        copies[7].wait()
        for k in range(4):
            xe_ref[k] = edge_row(adj_ref, k, row_e)
            xo_ref[k] = edge_row(adj_ref, k, row_o)
            ye_ref[k] = edge_col(adj_ref, k, col_e)
            yo_ref[k] = edge_col(adj_ref, k, col_o)

    def second(
        adj_hbm, vel_hbm, dif_hbm, con_hbm, rec_hbm, height_hbm, dst_hbm, arrived_ref,
        next_hbm, conc_ref, xe_ref, xo_ref, ye_ref, yo_ref,
        state_ref, vel_ref, dif_ref, con_ref, rec_ref, height_ref, dst_ref,
        pad_ref, fluid_ref, coef_ref, count_ref, wall_ref, next_ref, sem,
    ):
        copies = [
            pltpu.make_async_copy(height_hbm, height_ref, sem.at[0]),
            pltpu.make_async_copy(vel_hbm, vel_ref, sem.at[1]),
            pltpu.make_async_copy(dif_hbm, dif_ref, sem.at[2]),
            pltpu.make_async_copy(con_hbm, con_ref, sem.at[3]),
            pltpu.make_async_copy(rec_hbm, rec_ref, sem.at[4]),
            pltpu.make_async_copy(dst_hbm, dst_ref, sem.at[5]),
            pltpu.make_async_copy(adj_hbm, state_ref.at[:, inside[0], inside[1], :], sem.at[6]),
        ]
        start_all(copies)
        row_e, row_o, col_e, col_o = edges_at()
        clear_halo(pad_ref, range(4))
        clear_halo(state_ref, range(4))
        copies[0].wait()
        fluid_ref[...] = row_values(height_ref[...])
        wait_all(copies[1:4])
        fill_pads(pad_ref, vel_ref, dif_ref, con_ref)
        wait_all(copies[4:6])
        count_ref[...] = receptor_counts(rec_ref[...], cols)
        wall_ref[...] = scatter_blocks(dst_ref[...], arrived_ref[...], cols)
        coefficients(pad_ref, vel_ref, fluid_ref, coef_ref)
        copies[6].wait()
        state_ref[3, 1 : cx + 1, PADY : PADY + cy, :] += count_ref[...].reshape(cx, cy, 128)
        stencil(state_ref, coef_ref, ((3, count_ref), (2, wall_ref)), next_ref)
        out = pltpu.make_async_copy(next_ref, next_hbm, sem.at[7])
        out.start()
        conc_ref[...] = next_ref[3]
        for k in range(4):
            xe_ref[k] = edge_row(next_ref, k, row_e)
            xo_ref[k] = edge_row(next_ref, k, row_o)
            ye_ref[k] = edge_col(next_ref, k, col_e)
            yo_ref[k] = edge_col(next_ref, k, col_o)
        xe_ref[4] = fluid_ref[pl.ds(pl.multiple_of(row_e * cy, 8), cy), :]
        xo_ref[4] = fluid_ref[pl.ds(pl.multiple_of(row_o * cy, 8), cy), :]
        ye_ref[4] = fluid_ref[pl.ds(col_e, cx, stride=cy), :]
        yo_ref[4] = fluid_ref[pl.ds(col_o, cx, stride=cy), :]
        out.wait()

    def edge_signs():
        me_x, me_y = lax.axis_index("gx"), lax.axis_index("gy")
        sx = (1 - 2 * lax.rem(me_x, 2)).astype(F32)
        sy = (1 - 2 * lax.rem(me_y, 2)).astype(F32)
        wrap_x = jnp.logical_or(me_x == 0, me_x == nx - 1)
        wrap_y = jnp.logical_or(me_y == 0, me_y == ny - 1)
        return sx, sy, wrap_x, wrap_y

    def third(
        conc_in, oxe, oxo, oye, oyo, hxe, hxo, hye, hyo, pxe, pxo, pye, pyo, src_ref, weight_ref,
        blocks_ref, xe_ref, xo_ref, ye_ref, yo_ref,
        conc_ref, dxe, dxo, dye, dyo,
    ):
        row_e, row_o, col_e, col_o = edges_at()
        sx, sy, wrap_x, wrap_y = edge_signs()
        hot = select_rows(src_ref[...], cols)
        for own, halo, part, add, out, sign, wrap, axis in (
            (oxe, hxe, pxe, dxe, xe_ref, sx, None, 0),
            (oxo, hxo, pxo, dxo, xo_ref, -sx, wrap_x, 0),
            (oye, hye, pye, dye, ye_ref, sy, None, 1),
            (oyo, hyo, pyo, dyo, yo_ref, -sy, wrap_y, 1),
        ):
            e = part[4]
            if wrap is not None:
                e = jnp.where(wrap, 0.0, e)
            there = halo[5]
            near = e * (own[5] + there + sign * halo[4])
            far = e * there
            slope = e * (sign * halo[6])
            for k in range(4):
                value = near * halo[k] - far * own[k]
                if k == axis:
                    value = value - slope * own[3]
                add[k] = value
                out[k] = part[k] + value
        for k in range(4):
            for row, out, dx in ((row_e, xe_ref, dxe), (row_o, xo_ref, dxo)):
                for col, dy in ((col_e, dye), (col_o, dyo)):
                    out[k, pl.ds(col, 1), :] += dy[k, pl.ds(row, 1), :]
            for col, out in ((col_e, ye_ref), (col_o, yo_ref)):
                for row, dx in ((row_e, dxe), (row_o, dxo)):
                    out[k, pl.ds(row, 1), :] += dx[k, pl.ds(col, 1), :]
        conc_ref[...] = conc_in[...]
        conc_ref[pl.ds(pl.multiple_of(row_e * cy, 8), cy), :] = xe_ref[3]
        conc_ref[pl.ds(pl.multiple_of(row_o * cy, 8), cy), :] = xo_ref[3]
        conc_ref[pl.ds(col_e, cx, stride=cy), :] = ye_ref[3]
        conc_ref[pl.ds(col_o, cx, stride=cy), :] = yo_ref[3]
        picked = join3(jnp.dot(hot, split3(conc_ref[...]), preferred_element_type=F32))
        blocks_ref[...] = weight_ref[...] * picked

    def fourth(
        next_hbm, vel_hbm, dif_hbm, con_hbm, height_hbm, dst_hbm,
        hxe, hxo, hye, hyo, exe, exo, eye, eyo, arrived_ref,
        out_hbm, sxe_ref, sxo_ref, sye_ref, syo_ref, cxe_ref, cxo_ref, cye_ref, cyo_ref,
        state_ref, vel_ref, dif_ref, con_ref, height_ref, dst_ref,
        pad_ref, fluid_ref, coef_ref, wall_ref, last_ref, sem,
    ):
        copies = [
            pltpu.make_async_copy(height_hbm, height_ref, sem.at[0]),
            pltpu.make_async_copy(vel_hbm, vel_ref, sem.at[1]),
            pltpu.make_async_copy(dif_hbm, dif_ref, sem.at[2]),
            pltpu.make_async_copy(con_hbm, con_ref, sem.at[3]),
            pltpu.make_async_copy(dst_hbm, dst_ref, sem.at[4]),
            pltpu.make_async_copy(next_hbm, state_ref.at[:, inside[0], inside[1], :], sem.at[5]),
        ]
        start_all(copies)
        row_e, row_o, col_e, col_o = edges_at()
        clear_halo(state_ref, range(4))
        copies[0].wait()
        fluid_ref[...] = row_values(height_ref[...])
        wait_all(copies[1:4])
        fill_pads(pad_ref, vel_ref, dif_ref, con_ref)
        halo = (hxe, hxo, hye, hyo)
        take_halo(pad_ref, 0, 4, *halo, True, False)
        take_halo(pad_ref, 1, 4, *halo, False, True)
        take_halo(pad_ref, 2, 5, *halo, True, True)
        take_halo(pad_ref, 3, 6, *halo, True, True)
        copies[4].wait()
        wall_ref[...] = scatter_blocks(dst_ref[...], arrived_ref[...], cols)
        coefficients(pad_ref, vel_ref, fluid_ref, coef_ref)
        copies[5].wait()
        for k in range(4):
            state_ref[k, row_e + 1, PADY : PADY + cy, :] = exe[k]
            state_ref[k, row_o + 1, PADY : PADY + cy, :] = exo[k]
            for i in range(cx):
                state_ref[k, i + 1, pl.ds(PADY + col_e, 1), :] = eye[k, i : i + 1, :]
                state_ref[k, i + 1, pl.ds(PADY + col_o, 1), :] = eyo[k, i : i + 1, :]
        stencil(state_ref, coef_ref, ((2, wall_ref),), last_ref)
        out = pltpu.make_async_copy(last_ref, out_hbm, sem.at[6])
        out.start()
        tile_e = col_e // 8 * 8
        tile_o = col_o // 8 * 8
        for k in range(4):
            sxe_ref[k] = edge_row(last_ref, k, row_e)
            sxo_ref[k] = edge_row(last_ref, k, row_o)
            for i in range(cx):
                at_e = pl.ds(pl.multiple_of(i * cy + tile_e, 8), 8)
                at_o = pl.ds(pl.multiple_of(i * cy + tile_o, 8), 8)
                sye_ref[k, i] = last_ref[k, at_e, :]
                syo_ref[k, i] = last_ref[k, at_o, :]
        par_x = lax.rem(lax.axis_index("gx"), 2)
        par_y = lax.rem(lax.axis_index("gy"), 2)
        cxe_ref[...] = coef_ref[1 + par_x, pl.ds(pl.multiple_of(row_e * cy, 8), cy), :]
        cxo_ref[...] = coef_ref[2 - par_x, pl.ds(pl.multiple_of(row_o * cy, 8), cy), :]
        cye_ref[...] = edge_col(coef_ref, 3 + par_y, col_e)
        cyo_ref[...] = edge_col(coef_ref, 4 - par_y, col_o)
        out.wait()

    def fifth(
        last_hbm, sxe, sxo, sye, syo, cxe, cxo, cye, cyo, hxe, hxo, hye, hyo,
        out_hbm, txe, txo, tye, tyo, dye, dyo, sem,
    ):
        row_e, row_o, col_e, col_o = edges_at()
        _, _, wrap_x, wrap_y = edge_signs()
        near_e, near_o = cye[...], jnp.where(wrap_y, 0.0, cyo[...])
        tile_e = col_e // 8 * 8
        tile_o = col_o // 8 * 8
        for k in range(4):
            dye[k] = near_e * hye[k]
            dyo[k] = near_o * hyo[k]
            tye[k] = sye[k]
            tyo[k] = syo[k]
            for i in range(1, cx - 1):
                tye[k, i, pl.ds(col_e - tile_e, 1), :] += dye[k, i : i + 1, :]
                tyo[k, i, pl.ds(col_o - tile_o, 1), :] += dyo[k, i : i + 1, :]
        copies = [
            pltpu.make_async_copy(
                strip.at[:, pl.ds(1, cx - 2)],
                out_hbm.at[:, pl.ds(1, cx - 2), pl.ds(pl.multiple_of(tile, 8), 8), :],
                sem.at[n],
            )
            for n, (strip, tile) in enumerate(((tye, tile_e), (tyo, tile_o)))
        ]
        start_all(copies)
        near_e, near_o = cxe[...], jnp.where(wrap_x, 0.0, cxo[...])
        for k in range(4):
            txe[k] = sxe[k] + near_e * hxe[k]
            txo[k] = sxo[k] + near_o * hxo[k]
            for row, out in ((row_e, txe), (row_o, txo)):
                for col, dy in ((col_e, dye), (col_o, dyo)):
                    out[k, pl.ds(col, 1), :] += dy[k, pl.ds(row, 1), :]
        more = [
            pltpu.make_async_copy(strip, out_hbm.at[:, row], sem.at[n])
            for n, (strip, row) in enumerate(((txe, row_e), (txo, row_o)), 2)
        ]
        start_all(more)
        wait_all(copies + more)

    def sds(*shape):
        return jax.ShapeDtypeStruct(shape, F32)

    def vm(*shape, dtype=F32):
        return pltpu.VMEM(shape, dtype)

    def dma(count):
        return pltpu.SemaphoreType.DMA((count,))

    def call(body, name, ins, outs, shapes, scratch, cost, limit=24, **more):
        return pl.pallas_call(
            body,
            name=name,
            out_shape=shapes,
            in_specs=ins,
            out_specs=outs,
            scratch_shapes=scratch,
            compiler_params=pltpu.CompilerParams(vmem_limit_bytes=limit << 20),
            cost_estimate=pl.CostEstimate(flops=cost, bytes_accessed=cost, transcendentals=0),
            **more,
        )

    int_table = vm(owners, cap, dtype=jnp.int32)
    three = [vm(3, cx, cy, 128, dtype=BF16)] + [vm(cx, cy, 128, dtype=BF16)] * 2
    strips = (sds(4, cy, 128), sds(4, cy, 128), sds(4, cx, 128), sds(4, cx, 128))

    def kernels(rcp):
        line = vm(1, rcp, dtype=jnp.int32)
        height = vm(cx, cy, dtype=jnp.int32)
        one = call(
            first, "first", [HBM] * 7, (VMEM,) * 5,
            (sds(slots, 128), sds(7, cy, 128), sds(7, cy, 128), sds(7, cx, 128), sds(7, cx, 128)),
            [vm(4, cols, 128), vm(2, cx, cy, 128, dtype=BF16)] + three[1:]
            + [line, int_table, vm(slots, 128), vm(3, cols, 128), dma(8)],
            4 << 20,
        )
        two = call(
            second, "second", [HBM] * 7 + [VMEM], (HBM,) + (VMEM,) * 5,
            (
                sds(4, cols, 128), sds(cols, 128),
                sds(5, cy, 128), sds(5, cy, 128), sds(5, cx, 128), sds(5, cx, 128),
            ),
            [vm(4, px, py, 128)] + three + [line, height, int_table]
            + [vm(4, px, py, 128), vm(cols, 128), vm(10, cols, 128), vm(cols, 128),
               vm(cols, 128), vm(4, cols, 128), dma(8)],
            8 << 20,
        )
        three_ = call(
            third, "third", [VMEM] * 15, (VMEM,) * 5, (sds(slots, 128),) + strips,
            [vm(cols, 128), vm(4, cy, 128), vm(4, cy, 128), vm(4, cx, 128), vm(4, cx, 128)],
            3 << 20,
        )
        four = call(
            fourth, "fourth", [HBM] * 6 + [VMEM] * 9, (HBM,) + (VMEM,) * 8,
            (sds(4, cols, 128), sds(4, cy, 128), sds(4, cy, 128),
             sds(4, cx, 8, 128), sds(4, cx, 8, 128),
             sds(cy, 128), sds(cy, 128), sds(cx, 128), sds(cx, 128)),
            [vm(4, px, py, 128)] + three + [height, int_table]
            + [vm(4, px, py, 128), vm(cols, 128), vm(10, cols, 128), vm(cols, 128),
               vm(4, cols, 128), dma(7)],
            8 << 20,
        )
        five = call(
            fifth, "fifth", [HBM] + [VMEM] * 12, HBM, sds(4, cx, cy, 128),
            [vm(4, cy, 128), vm(4, cy, 128), vm(4, cx, 8, 128), vm(4, cx, 8, 128),
             vm(4, cx, 128), vm(4, cx, 128), dma(4)],
            2 << 20,
            input_output_aliases={0: 0},
        )
        return one, two, three_, four, five

    return kernels


def shards(
    adjoint, velocity, diffusivity, concentration, heights, receptors, face_src, face_dst, face_coef
):
    nx, ny = lax.axis_size("gx"), lax.axis_size("gy")
    cx, cy, levels = adjoint.shape[1:]
    owners, cap = face_src.shape[2:]
    kernels = make_kernels(nx, ny, cx, cy, owners, cap)
    first, second, third, fourth, fifth = kernels(receptors.shape[2])

    def pairs(count):
        even = [(i, i ^ 1) for i in range(count)]
        odd = [(i, (i + 1) % count) for i in range(1, count, 2)]
        return even, odd + [(j, i) for i, j in odd]

    x_even, x_odd = pairs(nx)
    y_even, y_odd = pairs(ny)

    def exchange(xe, xo, ye, yo):
        yo = lax.ppermute(yo, "gy", y_odd)
        xo = lax.ppermute(xo, "gx", x_odd)
        xe = lax.ppermute(xe, "gx", x_even)
        ye = lax.ppermute(ye, "gy", y_even)
        return xe, xo, ye, yo

    def deliver(blocks):
        sent = blocks.reshape(owners, cap, levels)
        got = lax.all_to_all(sent, "gx", split_axis=0, concat_axis=0, tiled=True)
        return got.reshape(owners * cap, levels)

    src = face_src.reshape(owners, cap)
    dst = face_dst.reshape(owners, cap)
    weight = face_coef.reshape(owners * cap, levels)
    line = receptors.reshape(1, -1)
    flat = adjoint.reshape(4, cx * cy, levels)
    pinned = [
        pltpu.with_memory_space_constraint(x, pltpu.HBM)
        for x in (flat, velocity, diffusivity, concentration, line, src, weight)
    ]
    blocks, *own = first(*pinned)
    arrived = deliver(blocks)
    halos = exchange(*own)
    inner, conc, *part = second(
        adjoint, velocity, diffusivity, concentration, line, heights, dst, arrived
    )
    blocks, *edges = third(conc, *own, *halos, *part, src, weight)
    arrived = deliver(blocks)
    later = exchange(*edges)
    last, *strips = fourth(
        inner.reshape(4, cx, cy, levels), velocity, diffusivity, concentration, heights, dst,
        *halos, *edges, arrived,
    )
    return fifth(last.reshape(4, cx, cy, levels), *strips, *later)


def solution(mesh):
    placed = (
        P(None, "gx", "gy", None),
        P(None, "gx", "gy", None),
        P("gx", "gy", None),
        P("gx", "gy", None),
        P("gx", "gy"),
        P("gx", "gy", None),
        P("gx", "gy", None, None),
        P("gx", "gy", None, None),
        P("gx", "gy", None, None, None),
    )
    return jax.shard_map(
        shards, mesh=mesh, in_specs=placed, out_specs=P(None, "gx", "gy", None), check_vma=False
    )
```

```python
import jax
import jax.numpy as jnp
from jax import lax
from jax.experimental import pallas as pl
from jax.experimental.pallas import tpu as pltpu
from jax.sharding import PartitionSpec as P

F32 = jnp.float32
BF16 = jnp.bfloat16
PADY = 8
VMEM = pl.BlockSpec(memory_space=pltpu.VMEM)
HBM = pl.BlockSpec(memory_space=pltpu.HBM)


def split3(x):
    hi = x.astype(BF16)
    rest = x - hi.astype(F32)
    mid = rest.astype(BF16)
    low = (rest - mid.astype(F32)).astype(BF16)
    return jnp.concatenate([hi, mid, low], axis=1)


def join3(x):
    return x[:, :128] + x[:, 128:256] + x[:, 256:384]


def row_values(table):
    n = table.shape[1]
    eye = lax.broadcasted_iota(jnp.int32, (n, n), 0) == lax.broadcasted_iota(jnp.int32, (n, n), 1)
    high = table >> 4
    low = table & 15
    ones = jnp.ones((n, 128), BF16)
    total = None
    for part in (high * 16, low):
        part = part.astype(F32)
        rows = [
            jnp.where(eye, jnp.broadcast_to(part[d : d + 1], (n, n)), 0.0)
            for d in range(table.shape[0])
        ]
        spread = jnp.concatenate(rows, axis=0).astype(BF16)
        value = jnp.dot(spread, ones, preferred_element_type=F32)
        total = value if total is None else total + value
    return total


def select_cols(table, cols):
    d_count, n = table.shape
    slots = d_count * n
    tile = (
        lax.broadcasted_iota(jnp.int32, (n, slots), 1) % n
        == lax.broadcasted_iota(jnp.int32, (n, slots), 0)
    ).astype(F32).astype(BF16)
    mine = (
        lax.broadcasted_iota(jnp.int32, (d_count, slots), 1) // n
        == lax.broadcasted_iota(jnp.int32, (d_count, slots), 0)
    )
    high = ((table >> 4) * 16).astype(F32).astype(BF16)
    low = (table & 15).astype(F32).astype(BF16)
    value = jnp.dot(high, tile, preferred_element_type=F32) + jnp.dot(
        low, tile, preferred_element_type=F32
    )
    line = jnp.sum(jnp.where(mine, value, 0.0), axis=0, keepdims=True).astype(jnp.int32)
    col = lax.broadcasted_iota(jnp.int32, (cols, slots), 0)
    return (col == line).astype(F32).astype(BF16)


def receptor_counts(line, cols):
    entries = line.shape[1]
    col = lax.broadcasted_iota(jnp.int32, (cols, entries), 0)
    level = lax.broadcasted_iota(jnp.int32, (128, entries), 0)
    hot_col = (col == (line >> 7)).astype(F32).astype(BF16)
    hot_level = (level == (line & 127)).astype(F32).astype(BF16)
    return lax.dot_general(
        hot_col, hot_level, (((1,), (1,)), ((), ())), preferred_element_type=F32
    )


def make_kernels(nx, ny, cx, cy, owners, cap):
    cols = cx * cy
    slots = owners * cap
    px, py = cx + 2, cy + 2 * PADY
    inside = (pl.ds(1, cx), pl.ds(PADY, cy))

    def edges_at():
        par_x = lax.rem(lax.axis_index("gx"), 2)
        par_y = lax.rem(lax.axis_index("gy"), 2)
        return (
            (cx - 1) * (1 - par_x), (cx - 1) * par_x,
            (cy - 1) * (1 - par_y), (cy - 1) * par_y,
        )

    def start_all(copies):
        for copy in copies:
            copy.start()

    def wait_all(copies):
        for copy in copies:
            copy.wait()

    def clear_halo(pad_ref, planes):
        zero = jnp.zeros((px, PADY, 128), F32)
        row = jnp.zeros((cy, 128), F32)
        for k in planes:
            pad_ref[k, :, 0:PADY, :] = zero
            pad_ref[k, :, PADY + cy : py, :] = zero
            pad_ref[k, 0, PADY : PADY + cy, :] = row
            pad_ref[k, cx + 1, PADY : PADY + cy, :] = row

    def take_halo(pad_ref, plane, n, xe_ref, xo_ref, ye_ref, yo_ref, with_x, with_y):
        me_x, me_y = lax.axis_index("gx"), lax.axis_index("gy")
        par_x, par_y = lax.rem(me_x, 2), lax.rem(me_y, 2)
        if with_x:
            e, o = xe_ref[n], xo_ref[n]
            before = jnp.where(par_x == 0, o, e)
            after = jnp.where(par_x == 0, e, o)
            pad_ref[plane, 0, PADY : PADY + cy, :] = jnp.where(me_x == 0, 0.0, before)
            pad_ref[plane, cx + 1, PADY : PADY + cy, :] = jnp.where(me_x == nx - 1, 0.0, after)
        if with_y:
            e, o = ye_ref[n], yo_ref[n]
            before = jnp.where(me_y == 0, 0.0, jnp.where(par_y == 0, o, e))
            after = jnp.where(me_y == ny - 1, 0.0, jnp.where(par_y == 0, e, o))
            for i in range(cx):
                pad_ref[plane, i + 1, PADY - 1 : PADY, :] = before[i : i + 1]
                pad_ref[plane, i + 1, PADY + cy : PADY + cy + 1, :] = after[i : i + 1]

    def fill_pads(pad_ref, vel_ref, dif_ref, con_ref=None):
        pad_ref[0, 1 : cx + 1, PADY : PADY + cy, :] = vel_ref[0].astype(F32)
        pad_ref[1, 1 : cx + 1, PADY : PADY + cy, :] = vel_ref[1].astype(F32)
        pad_ref[2, 1 : cx + 1, PADY : PADY + cy, :] = dif_ref[...].astype(F32)
        if con_ref is not None:
            pad_ref[3, 1 : cx + 1, PADY : PADY + cy, :] = con_ref[...].astype(F32)

    def cell_coefficients(i, jv, uz, pad_ref, fluid_ref):
        lane = lax.broadcasted_iota(jnp.int32, (8, 128), 1)
        top = lane == 127
        bottom = lane == 0

        def up(x):
            return jnp.where(top, 0.0, pltpu.roll(x, 127, axis=1))

        def down(x):
            return jnp.where(bottom, 0.0, pltpu.roll(x, 1, axis=1))

        j = PADY + 8 * jv
        at = pl.ds(i * cy + 8 * jv, 8)
        fluid = (lane.astype(F32) >= fluid_ref[at, :]).astype(F32)
        e = 0.05 * fluid
        k0 = pad_ref[2, i + 1, j : j + 8, :]
        ends = None
        out = [None]
        for plane, sign, a, b in (
            (0, 1.0, i + 2, j), (0, -1.0, i, j), (1, 1.0, i + 1, j + 1), (1, -1.0, i + 1, j - 1),
        ):
            kn = k0 + pad_ref[2, a, b : b + 8, :]
            un = pad_ref[plane, a, b : b + 8, :]
            out.append(e * (kn + un if sign > 0 else kn - un))
            ends = kn if ends is None else ends + kn
        kn = k0 + up(k0)
        ends = ends + kn
        out.append(jnp.where(top, 0.0, e * (kn + up(uz))))
        kn = k0 + down(k0)
        ends = ends + kn
        out.append(jnp.where(bottom, 0.0, e * (kn - down(uz))))
        out[0] = fluid - e * ends
        return out, e

    def cell_gradients(i, jv, e, pad_ref):
        lane = lax.broadcasted_iota(jnp.int32, (8, 128), 1)
        j = PADY + 8 * jv
        c0 = pad_ref[3, i + 1, j : j + 8, :]
        above = jnp.where(lane == 127, 0.0, pltpu.roll(c0, 127, axis=1))
        below = jnp.where(lane == 0, 0.0, pltpu.roll(c0, 1, axis=1))
        return [
            e * (pad_ref[3, i + 2, j : j + 8, :] - pad_ref[3, i, j : j + 8, :]),
            e * (pad_ref[3, i + 1, j + 1 : j + 9, :] - pad_ref[3, i + 1, j - 1 : j + 7, :]),
            e * (above - below),
        ]

    def cells():
        return [(i, jv) for i in range(cx) for jv in range(cy // 8)]

    def vertical(vel_ref, i, jv):
        pair = vel_ref[2, i, 16 * (jv // 2) : 16 * (jv // 2) + 16, :].astype(F32)
        return pair[8 * (jv % 2) : 8 * (jv % 2) + 8]

    def cell_step(i, jv, c, state_ref, k):
        j = PADY + 8 * jv
        f = state_ref[k, i + 1, j : j + 8, :]
        value = c[0] * f
        value = value + c[1] * state_ref[k, i + 2, j : j + 8, :]
        value = value + c[2] * state_ref[k, i, j : j + 8, :]
        value = value + c[3] * state_ref[k, i + 1, j + 1 : j + 9, :]
        value = value + c[4] * state_ref[k, i + 1, j - 1 : j + 7, :]
        value = value + c[5] * pltpu.roll(f, 127, axis=1)
        value = value + c[6] * pltpu.roll(f, 1, axis=1)
        return value

    def edge_row(ref, k, row):
        return ref[k, pl.ds(pl.multiple_of(row * cy, 8), cy), :]

    def edge_col(ref, k, col):
        return ref[k, pl.ds(col, cx, stride=cy), :]

    def first(
        adj_hbm, vel_hbm, dif_hbm, con_hbm, rec_hbm,
        xe_ref, xo_ref, ye_ref, yo_ref,
        adj_ref, vel_ref, dif_ref, con_ref, rec_ref, side_ref, sem,
    ):
        copies = [
            pltpu.make_async_copy(rec_hbm, rec_ref, sem.at[0]),
            pltpu.make_async_copy(vel_hbm.at[pl.ds(0, 2)], vel_ref, sem.at[1]),
            pltpu.make_async_copy(dif_hbm, dif_ref, sem.at[2]),
            pltpu.make_async_copy(con_hbm, con_ref, sem.at[3]),
            pltpu.make_async_copy(adj_hbm, adj_ref, sem.at[4]),
        ]
        start_all(copies)
        row_e, row_o, col_e, col_o = edges_at()
        copies[0].wait()
        counts = receptor_counts(rec_ref[...], cols)
        wait_all(copies[1:4])
        side_ref[0] = vel_ref[1].astype(F32).reshape(cols, 128)
        side_ref[1] = dif_ref[...].astype(F32).reshape(cols, 128)
        side_ref[2] = con_ref[...].astype(F32).reshape(cols, 128)
        for row, out in ((row_e, xe_ref), (row_o, xo_ref)):
            out[4] = vel_ref[0, row].astype(F32)
            out[5] = dif_ref[row].astype(F32)
            out[6] = con_ref[row].astype(F32)
        for col, out in ((col_e, ye_ref), (col_o, yo_ref)):
            for k in range(3):
                out[4 + k] = edge_col(side_ref, k, col)
        copies[4].wait()
        adj_ref[3] += counts
        for k in range(4):
            xe_ref[k] = edge_row(adj_ref, k, row_e)
            xo_ref[k] = edge_row(adj_ref, k, row_o)
            ye_ref[k] = edge_col(adj_ref, k, col_e)
            yo_ref[k] = edge_col(adj_ref, k, col_o)

    def second(
        adj_hbm, vel_hbm, dif_hbm, rec_hbm, height_hbm, src_hbm, weight_hbm,
        now_ref, soon_ref, hot_ref, weight_ref, exe_ref, exo_ref, eye_ref, eyo_ref,
        state_ref, vel_ref, dif_ref, rec_ref, height_ref, src_ref,
        pad_ref, fluid_ref, count_ref, next_ref, sem,
    ):
        copies = [
            pltpu.make_async_copy(src_hbm, src_ref, sem.at[0]),
            pltpu.make_async_copy(height_hbm, height_ref, sem.at[1]),
            pltpu.make_async_copy(rec_hbm, rec_ref, sem.at[2]),
            pltpu.make_async_copy(dif_hbm, dif_ref, sem.at[3]),
            pltpu.make_async_copy(
                adj_hbm.at[3], state_ref.at[0, inside[0], inside[1], :], sem.at[4]
            ),
            pltpu.make_async_copy(vel_hbm, vel_ref, sem.at[5]),
            pltpu.make_async_copy(weight_hbm, weight_ref, sem.at[6]),
        ]
        start_all(copies)
        row_e, row_o, col_e, col_o = edges_at()
        clear_halo(pad_ref, range(3))
        clear_halo(state_ref, range(1))
        copies[0].wait()
        index = row_values(src_ref[...]).astype(jnp.int32)
        copies[1].wait()
        fluid_ref[...] = row_values(height_ref[...])
        copies[2].wait()
        count_ref[...] = receptor_counts(rec_ref[...], cols)
        wait_all(copies[3:6])
        fill_pads(pad_ref, vel_ref, dif_ref)
        state_ref[0, 1 : cx + 1, PADY : PADY + cy, :] += count_ref[...].reshape(cx, cy, 128)
        for i, jv in cells():
            at = pl.ds(i * cy + 8 * jv, 8)
            c, e = cell_coefficients(i, jv, vertical(vel_ref, i, jv), pad_ref, fluid_ref)
            fluid_ref[at, :] = e
            next_ref[at, :] = cell_step(i, jv, c, state_ref, 0) + count_ref[at, :]
        lane = lax.broadcasted_iota(jnp.int32, index.shape, 1)
        i, j = index // cy, index % cy
        near = jnp.logical_or(
            jnp.logical_or(
                jnp.logical_and(i == row_e, j == lane),
                jnp.logical_and(i == row_o, j + cy == lane),
            ),
            jnp.logical_or(
                jnp.logical_and(j == col_e, i + 2 * cy == lane),
                jnp.logical_and(j == col_o, i + 2 * cy + cx == lane),
            ),
        )
        hot_ref[...] = jnp.where(jnp.logical_and(near, index >= 0), 1.0, 0.0).astype(BF16)
        hot = [(index == lane + t).astype(F32).astype(BF16) for t in range(0, cols, 128)]
        hot = jnp.concatenate(hot, axis=1)
        copies[6].wait()
        weight = weight_ref[...]
        conc = state_ref[0, 1 : cx + 1, PADY : PADY + cy, :].reshape(cols, 128)
        both = jnp.concatenate([split3(conc), split3(next_ref[...])], axis=1)
        picked = jnp.dot(hot, both, preferred_element_type=F32)
        now_ref[...] = weight * join3(picked[:, :384])
        soon_ref[...] = weight * join3(picked[:, 384:])
        exe_ref[...] = fluid_ref[pl.ds(pl.multiple_of(row_e * cy, 8), cy), :]
        exo_ref[...] = fluid_ref[pl.ds(pl.multiple_of(row_o * cy, 8), cy), :]
        eye_ref[...] = fluid_ref[pl.ds(col_e, cx, stride=cy), :]
        eyo_ref[...] = fluid_ref[pl.ds(col_o, cx, stride=cy), :]

    def edge_signs():
        me_x, me_y = lax.axis_index("gx"), lax.axis_index("gy")
        sx = (1 - 2 * lax.rem(me_x, 2)).astype(F32)
        sy = (1 - 2 * lax.rem(me_y, 2)).astype(F32)
        wrap_x = jnp.logical_or(me_x == 0, me_x == nx - 1)
        wrap_y = jnp.logical_or(me_y == 0, me_y == ny - 1)
        return sx, sy, wrap_x, wrap_y

    def edge_terms(own, halo, e, sign, wrap):
        e = e[...]
        if wrap is not None:
            e = jnp.where(wrap, 0.0, e)
        there = halo[5]
        return e * ((own[5] + there + sign * halo[4]) * halo[3] - there * own[3])

    def third(
        oxe, oxo, oye, oyo, hxe, hxo, hye, hyo, exe, exo, eye, eyo,
        now_ref, soon_ref, hot_ref, weight_ref, blocks_ref,
    ):
        sx, sy, wrap_x, wrap_y = edge_signs()
        edges = [
            edge_terms(oxe, hxe, exe, sx, None),
            edge_terms(oxo, hxo, exo, -sx, wrap_x),
            edge_terms(oye, hye, eye, sy, None),
            edge_terms(oyo, hyo, eyo, -sy, wrap_y),
        ]
        used = 2 * (cx + cy)
        edges = jnp.concatenate(edges + [jnp.zeros((128 - used, 128), F32)], axis=0)
        more = join3(jnp.dot(hot_ref[...], split3(edges), preferred_element_type=F32))
        blocks_ref[:, 0:cap, :] = now_ref[...].reshape(owners, cap, 128)
        soon = soon_ref[...] + weight_ref[...] * more
        blocks_ref[:, cap : 2 * cap, :] = soon.reshape(owners, cap, 128)

    def fourth(
        adj_hbm, vel_hbm, dif_hbm, con_hbm, rec_hbm, height_hbm, dst_hbm, hxe, hxo, hye, hyo,
        last_hbm, coef_hbm, hot_ref, xe_ref, xo_ref, ye_ref, yo_ref,
        cxe_ref, cxo_ref, cye_ref, cyo_ref,
        state_ref, vel_ref, dif_ref, con_ref, rec_ref, height_ref, dst_ref,
        pad_ref, fluid_ref, count_ref, coef_ref, next_ref, flat_ref, last_ref, sem,
    ):
        copies = [
            pltpu.make_async_copy(height_hbm, height_ref, sem.at[0]),
            pltpu.make_async_copy(vel_hbm, vel_ref, sem.at[1]),
            pltpu.make_async_copy(dif_hbm, dif_ref, sem.at[2]),
            pltpu.make_async_copy(con_hbm, con_ref, sem.at[3]),
            pltpu.make_async_copy(dst_hbm, dst_ref, sem.at[4]),
            pltpu.make_async_copy(rec_hbm, rec_ref, sem.at[5]),
            pltpu.make_async_copy(adj_hbm, state_ref.at[:, inside[0], inside[1], :], sem.at[6]),
        ]
        start_all(copies)
        row_e, row_o, col_e, col_o = edges_at()
        clear_halo(next_ref, range(4))
        halo = (hxe, hxo, hye, hyo)
        take_halo(pad_ref, 0, 4, *halo, True, False)
        take_halo(pad_ref, 1, 4, *halo, False, True)
        take_halo(pad_ref, 2, 5, *halo, True, True)
        take_halo(pad_ref, 3, 6, *halo, True, True)
        for k in range(4):
            take_halo(state_ref, k, k, *halo, True, True)
        copies[0].wait()
        fluid_ref[...] = row_values(height_ref[...])
        wait_all(copies[1:4])
        fill_pads(pad_ref, vel_ref, dif_ref, con_ref)
        wait_all(copies[4:7])
        hot_ref[...] = select_cols(dst_ref[...], cols)
        count_ref[...] = receptor_counts(rec_ref[...], cols)
        state_ref[3, 1 : cx + 1, PADY : PADY + cy, :] += count_ref[...].reshape(cx, cy, 128)
        for i, jv in cells():
            at = pl.ds(i * cy + 8 * jv, 8)
            j = PADY + 8 * jv
            c, e = cell_coefficients(i, jv, vertical(vel_ref, i, jv), pad_ref, fluid_ref)
            c = c + cell_gradients(i, jv, e, pad_ref)
            for n in range(10):
                coef_ref[n, at, :] = c[n]
            conc = state_ref[3, i + 1, j : j + 8, :]
            for k in range(4):
                value = cell_step(i, jv, c, state_ref, k)
                value = value + count_ref[at, :] if k == 3 else value - c[7 + k] * conc
                next_ref[k, i + 1, j : j + 8, :] = value
                flat_ref[k, at, :] = value
        outs = [pltpu.make_async_copy(coef_ref.at[pl.ds(0, 7)], coef_hbm, sem.at[7])]
        outs[0].start()
        for k in range(4):
            xe_ref[k] = edge_row(flat_ref, k, row_e)
            xo_ref[k] = edge_row(flat_ref, k, row_o)
            ye_ref[k] = edge_col(flat_ref, k, col_e)
            yo_ref[k] = edge_col(flat_ref, k, col_o)
        for i, jv in cells():
            at = pl.ds(i * cy + 8 * jv, 8)
            j = PADY + 8 * jv
            c = [coef_ref[n, at, :] for n in range(10)]
            conc = next_ref[3, i + 1, j : j + 8, :]
            for k in range(4):
                value = cell_step(i, jv, c, next_ref, k)
                if k < 3:
                    value = value - c[7 + k] * conc
                last_ref[k, i, 8 * jv : 8 * jv + 8, :] = value
        outs.append(pltpu.make_async_copy(last_ref, last_hbm, sem.at[8]))
        outs[1].start()
        par_x = lax.rem(lax.axis_index("gx"), 2)
        par_y = lax.rem(lax.axis_index("gy"), 2)
        cxe_ref[...] = coef_ref[1 + par_x, pl.ds(pl.multiple_of(row_e * cy, 8), cy), :]
        cxo_ref[...] = coef_ref[2 - par_x, pl.ds(pl.multiple_of(row_o * cy, 8), cy), :]
        cye_ref[...] = edge_col(coef_ref, 3 + par_y, col_e)
        cyo_ref[...] = edge_col(coef_ref, 4 - par_y, col_o)
        wait_all(outs)

    def fifth(
        arrived_ref, hot_ref, xe_in, xo_in, ye_in, yo_in,
        wall_ref, xe_ref, xo_ref, ye_ref, yo_ref,
    ):
        row_e, row_o, col_e, col_o = edges_at()
        blocks = split3(arrived_ref[:, 0:cap, :].reshape(slots, 128))
        wall_ref[0] = join3(jnp.dot(hot_ref[...], blocks, preferred_element_type=F32))
        xe_ref[...] = xe_in[...]
        xo_ref[...] = xo_in[...]
        ye_ref[...] = ye_in[...]
        yo_ref[...] = yo_in[...]
        xe_ref[2] += edge_row(wall_ref, 0, row_e)
        xo_ref[2] += edge_row(wall_ref, 0, row_o)
        ye_ref[2] += edge_col(wall_ref, 0, col_e)
        yo_ref[2] += edge_col(wall_ref, 0, col_o)

    def sixth(
        last_hbm, coef_hbm, wall_ref, arrived_ref, hot_ref,
        out_hbm, sxe_ref, sxo_ref, sye_ref, syo_ref,
        coef_ref, pad_ref, final_ref, add_ref, sem,
    ):
        row_e, row_o, col_e, col_o = edges_at()
        tile_e = pl.ds(pl.multiple_of(col_e // 8 * 8, 8), 8)
        tile_o = pl.ds(pl.multiple_of(col_o // 8 * 8, 8), 8)
        copies = [
            pltpu.make_async_copy(last_hbm.at[2], final_ref, sem.at[0]),
            pltpu.make_async_copy(coef_hbm, coef_ref, sem.at[1]),
            pltpu.make_async_copy(last_hbm.at[:, row_e], sxe_ref, sem.at[2]),
            pltpu.make_async_copy(last_hbm.at[:, row_o], sxo_ref, sem.at[3]),
            pltpu.make_async_copy(last_hbm.at[:, :, tile_e, :], sye_ref, sem.at[4]),
            pltpu.make_async_copy(last_hbm.at[:, :, tile_o, :], syo_ref, sem.at[5]),
        ]
        start_all(copies)
        blocks = split3(arrived_ref[:, cap : 2 * cap, :].reshape(slots, 128))
        add_ref[...] = join3(jnp.dot(hot_ref[...], blocks, preferred_element_type=F32))
        clear_halo(pad_ref, (0,))
        pad_ref[0, 1 : cx + 1, PADY : PADY + cy, :] = wall_ref[0].reshape(cx, cy, 128)
        wait_all(copies)
        for i, jv in cells():
            at = pl.ds(i * cy + 8 * jv, 8)
            c = [coef_ref[n, at, :] for n in range(7)]
            value = final_ref[i, 8 * jv : 8 * jv + 8, :] + add_ref[at, :]
            final_ref[i, 8 * jv : 8 * jv + 8, :] = value + cell_step(i, jv, c, pad_ref, 0)
        copy = pltpu.make_async_copy(final_ref, out_hbm.at[2], sem.at[6])
        copy.start()
        sxe_ref[2] = final_ref[row_e]
        sxo_ref[2] = final_ref[row_o]
        sye_ref[2] = final_ref[:, tile_e, :]
        syo_ref[2] = final_ref[:, tile_o, :]
        copy.wait()

    def seventh(
        last_hbm, sxe, sxo, sye, syo, cxe, cxo, cye, cyo, hxe, hxo, hye, hyo,
        out_hbm, txe, txo, tye, tyo, dye, dyo, sem,
    ):
        row_e, row_o, col_e, col_o = edges_at()
        _, _, wrap_x, wrap_y = edge_signs()
        near_e, near_o = cye[...], jnp.where(wrap_y, 0.0, cyo[...])
        tile_e = col_e // 8 * 8
        tile_o = col_o // 8 * 8
        for k in range(4):
            dye[k] = near_e * hye[k]
            dyo[k] = near_o * hyo[k]
            tye[k] = sye[k]
            tyo[k] = syo[k]
            for i in range(1, cx - 1):
                tye[k, i, pl.ds(col_e - tile_e, 1), :] += dye[k, i : i + 1, :]
                tyo[k, i, pl.ds(col_o - tile_o, 1), :] += dyo[k, i : i + 1, :]
        copies = [
            pltpu.make_async_copy(
                strip.at[:, pl.ds(1, cx - 2)],
                out_hbm.at[:, pl.ds(1, cx - 2), pl.ds(pl.multiple_of(tile, 8), 8), :],
                sem.at[n],
            )
            for n, (strip, tile) in enumerate(((tye, tile_e), (tyo, tile_o)))
        ]
        start_all(copies)
        near_e, near_o = cxe[...], jnp.where(wrap_x, 0.0, cxo[...])
        for k in range(4):
            txe[k] = sxe[k] + near_e * hxe[k]
            txo[k] = sxo[k] + near_o * hxo[k]
            for row, out in ((row_e, txe), (row_o, txo)):
                for col, dy in ((col_e, dye), (col_o, dyo)):
                    out[k, pl.ds(col, 1), :] += dy[k, pl.ds(row, 1), :]
        more = [
            pltpu.make_async_copy(strip, out_hbm.at[:, row], sem.at[n])
            for n, (strip, row) in enumerate(((txe, row_e), (txo, row_o)), 2)
        ]
        start_all(more)
        wait_all(copies + more)

    def sds(*shape):
        return jax.ShapeDtypeStruct(shape, F32)

    def hbm(*shape):
        return pltpu.HBM(shape, F32)

    def vm(*shape, dtype=F32):
        return pltpu.VMEM(shape, dtype)

    def dma(count):
        return pltpu.SemaphoreType.DMA((count,))

    def call(body, name, ins, outs, shapes, scratch, cost, limit=24, **more):
        return pl.pallas_call(
            body,
            name=name,
            out_shape=shapes,
            in_specs=ins,
            out_specs=outs,
            scratch_shapes=scratch,
            compiler_params=pltpu.CompilerParams(vmem_limit_bytes=limit << 20),
            cost_estimate=pl.CostEstimate(flops=cost, bytes_accessed=cost, transcendentals=0),
            **more,
        )

    int_table = vm(owners, cap, dtype=jnp.int32)
    three = [vm(3, cx, cy, 128, dtype=BF16)] + [vm(cx, cy, 128, dtype=BF16)] * 2
    strips = (sds(4, cy, 128), sds(4, cy, 128), sds(4, cx, 128), sds(4, cx, 128))
    sides = (sds(cy, 128), sds(cy, 128), sds(cx, 128), sds(cx, 128))
    height = vm(cx, cy, dtype=jnp.int32)
    padded = vm(4, px, py, 128)

    def kernels(rcp):
        line = vm(1, rcp, dtype=jnp.int32)
        return (
            call(
                first, "first", [HBM] * 5, (VMEM,) * 4,
                (sds(7, cy, 128), sds(7, cy, 128), sds(7, cx, 128), sds(7, cx, 128)),
                [vm(4, cols, 128), vm(2, cx, cy, 128, dtype=BF16)] + three[1:]
                + [line, vm(3, cols, 128), dma(5)],
                4 << 20,
            ),
            call(
                second, "second", [HBM] * 7, (VMEM,) * 8,
                (sds(slots, 128), sds(slots, 128),
                 jax.ShapeDtypeStruct((slots, 128), BF16), sds(slots, 128)) + sides,
                [vm(1, px, py, 128)] + three[:2] + [line, height, int_table]
                + [vm(3, px, py, 128), vm(cols, 128), vm(cols, 128), vm(cols, 128), dma(7)],
                8 << 20,
            ),
            call(
                third, "third", [VMEM] * 16, VMEM, sds(owners, 2 * cap, 128), [], 2 << 20,
            ),
            call(
                fourth, "fourth", [HBM] * 7 + [VMEM] * 4, (HBM,) * 2 + (VMEM,) * 9,
                (hbm(4, cx, cy, 128), hbm(7, cols, 128), jax.ShapeDtypeStruct((cols, slots), BF16))
                + strips + sides,
                [padded] + three + [line, height, int_table]
                + [padded, vm(cols, 128), vm(cols, 128), vm(10, cols, 128), padded,
                   vm(4, cols, 128), vm(4, cx, cy, 128), dma(9)],
                10 << 20,
            ),
            call(
                fifth, "fifth", [VMEM] * 6, (VMEM,) * 5, (sds(1, cols, 128),) + strips, [],
                2 << 20,
            ),
            call(
                sixth, "sixth", [HBM] * 2 + [VMEM] * 3, (HBM,) + (VMEM,) * 4,
                (hbm(4, cx, cy, 128), sds(4, cy, 128), sds(4, cy, 128),
                 sds(4, cx, 8, 128), sds(4, cx, 8, 128)),
                [vm(7, cols, 128), vm(1, px, py, 128), vm(cx, cy, 128), vm(cols, 128), dma(7)],
                5 << 20,
                input_output_aliases={0: 0},
            ),
            call(
                seventh, "seventh", [HBM] + [VMEM] * 12, HBM, sds(4, cx, cy, 128),
                [vm(4, cy, 128), vm(4, cy, 128), vm(4, cx, 8, 128), vm(4, cx, 8, 128),
                 vm(4, cx, 128), vm(4, cx, 128), dma(4)],
                2 << 20,
                input_output_aliases={0: 0},
            ),
        )

    return kernels


def shards(
    adjoint, velocity, diffusivity, concentration, heights, receptors, face_src, face_dst, face_coef
):
    nx, ny = lax.axis_size("gx"), lax.axis_size("gy")
    cx, cy, levels = adjoint.shape[1:]
    owners, cap = face_src.shape[2:]
    kernels = make_kernels(nx, ny, cx, cy, owners, cap)
    first, second, third, fourth, fifth, sixth, seventh = kernels(receptors.shape[2])

    def swap(partner):
        return [
            (x * ny + y, px * ny + py)
            for x in range(nx) for y in range(ny) for px, py in (partner(x, y),)
        ]

    def odd(i):
        return i - 1 if i % 2 == 0 else i + 1

    x_even = swap(lambda x, y: (x ^ 1, y))
    x_odd = swap(lambda x, y: (odd(x), y) if 0 < x < nx - 1 else (x, y ^ 1))
    y_even = swap(lambda x, y: (x, y ^ 1))
    y_odd = swap(lambda x, y: (x, odd(y)) if 0 < y < ny - 1 else (x ^ 1, y))

    def exchange(*edges):
        swaps = (x_even, x_odd, y_even, y_odd)
        return [lax.ppermute(e, ("gx", "gy"), pairs) for e, pairs in zip(edges, swaps)]

    src = face_src.reshape(owners, cap)
    dst = face_dst.reshape(owners, cap)
    weight = face_coef.reshape(owners * cap, levels)
    line = receptors.reshape(1, -1)
    flat = adjoint.reshape(4, cx * cy, levels)

    def pinned(*arrays):
        return [pltpu.with_memory_space_constraint(x, pltpu.HBM) for x in arrays]

    own = first(*pinned(flat, velocity, diffusivity, concentration, line))
    halos = exchange(*own)
    now, soon, hot, weight, *fluid = second(
        *pinned(adjoint), velocity, *pinned(diffusivity, line, heights, src, weight)
    )
    blocks = third(*own, *halos, *fluid, now, soon, hot, weight)
    arrived = lax.all_to_all(blocks, "gx", split_axis=0, concat_axis=0, tiled=True)
    last, coefs, hot, *rest = fourth(
        *pinned(adjoint), velocity, diffusivity, concentration, *pinned(line, heights, dst), *halos
    )
    edges, sides = rest[:4], rest[4:]
    wall, *edges = fifth(arrived, hot, *edges)
    halos = exchange(*edges)
    out, *strips = sixth(*pinned(last, coefs), wall, arrived, hot)
    return seventh(*pinned(out), *strips, *sides, *halos)


def solution(mesh):
    placed = (
        P(None, "gx", "gy", None),
        P(None, "gx", "gy", None),
        P("gx", "gy", None),
        P("gx", "gy", None),
        P("gx", "gy"),
        P("gx", "gy", None),
        P("gx", "gy", None, None),
        P("gx", "gy", None, None),
        P("gx", "gy", None, None, None),
    )
    return jax.shard_map(
        shards, mesh=mesh, in_specs=placed, out_specs=P(None, "gx", "gy", None), check_vma=False
    )
```

```python
import jax
import jax.numpy as jnp
from jax import lax
from jax.experimental import pallas as pl
from jax.experimental.pallas import tpu as pltpu
from jax.sharding import PartitionSpec as P

F32 = jnp.float32
BF16 = jnp.bfloat16
PADY = 8
VMEM = pl.BlockSpec(memory_space=pltpu.VMEM)
HBM = pl.BlockSpec(memory_space=pltpu.HBM)


def split3(x):
    hi = x.astype(BF16)
    rest = x - hi.astype(F32)
    mid = rest.astype(BF16)
    low = (rest - mid.astype(F32)).astype(BF16)
    return jnp.concatenate([hi, mid, low], axis=1)


def join3(x):
    return x[:, :128] + x[:, 128:256] + x[:, 256:384]


def row_values(table):
    n = table.shape[1]
    eye = lax.broadcasted_iota(jnp.int32, (n, n), 0) == lax.broadcasted_iota(jnp.int32, (n, n), 1)
    high = table >> 4
    low = table & 15
    ones = jnp.ones((n, 128), BF16)
    total = None
    for part in (high * 16, low):
        part = part.astype(F32)
        rows = [
            jnp.where(eye, jnp.broadcast_to(part[d : d + 1], (n, n)), 0.0)
            for d in range(table.shape[0])
        ]
        spread = jnp.concatenate(rows, axis=0).astype(BF16)
        value = jnp.dot(spread, ones, preferred_element_type=F32)
        total = value if total is None else total + value
    return total


def select_cols(table, cols):
    d_count, n = table.shape
    slots = d_count * n
    tile = (
        lax.broadcasted_iota(jnp.int32, (n, slots), 1) % n
        == lax.broadcasted_iota(jnp.int32, (n, slots), 0)
    ).astype(F32).astype(BF16)
    mine = (
        lax.broadcasted_iota(jnp.int32, (d_count, slots), 1) // n
        == lax.broadcasted_iota(jnp.int32, (d_count, slots), 0)
    )
    high = ((table >> 4) * 16).astype(F32).astype(BF16)
    low = (table & 15).astype(F32).astype(BF16)
    value = jnp.dot(high, tile, preferred_element_type=F32) + jnp.dot(
        low, tile, preferred_element_type=F32
    )
    line = jnp.sum(jnp.where(mine, value, 0.0), axis=0, keepdims=True).astype(jnp.int32)
    col = lax.broadcasted_iota(jnp.int32, (cols, slots), 0)
    return (col == line).astype(F32).astype(BF16)


def receptor_counts(line, cols):
    entries = line.shape[1]
    col = lax.broadcasted_iota(jnp.int32, (cols, entries), 0)
    level = lax.broadcasted_iota(jnp.int32, (128, entries), 0)
    hot_col = (col == (line >> 7)).astype(F32).astype(BF16)
    hot_level = (level == (line & 127)).astype(F32).astype(BF16)
    return lax.dot_general(
        hot_col, hot_level, (((1,), (1,)), ((), ())), preferred_element_type=F32
    )


def make_kernels(nx, ny, cx, cy, owners, cap):
    cols = cx * cy
    slots = owners * cap
    px, py = cx + 2, cy + 2 * PADY
    inside = (pl.ds(1, cx), pl.ds(PADY, cy))

    def edges_at():
        par_x = lax.rem(lax.axis_index("gx"), 2)
        par_y = lax.rem(lax.axis_index("gy"), 2)
        return (
            (cx - 1) * (1 - par_x), (cx - 1) * par_x,
            (cy - 1) * (1 - par_y), (cy - 1) * par_y,
        )

    def start_all(copies):
        for copy in copies:
            copy.start()

    def wait_all(copies):
        for copy in copies:
            copy.wait()

    def clear_halo(pad_ref, planes):
        zero = jnp.zeros((px, PADY, 128), F32)
        row = jnp.zeros((cy, 128), F32)
        for k in planes:
            pad_ref[k, :, 0:PADY, :] = zero
            pad_ref[k, :, PADY + cy : py, :] = zero
            pad_ref[k, 0, PADY : PADY + cy, :] = row
            pad_ref[k, cx + 1, PADY : PADY + cy, :] = row

    def take_halo(pad_ref, plane, n, xe_ref, xo_ref, ye_ref, yo_ref, with_x, with_y):
        me_x, me_y = lax.axis_index("gx"), lax.axis_index("gy")
        par_x, par_y = lax.rem(me_x, 2), lax.rem(me_y, 2)
        if with_x:
            e, o = xe_ref[n], xo_ref[n]
            before = jnp.where(par_x == 0, o, e)
            after = jnp.where(par_x == 0, e, o)
            pad_ref[plane, 0, PADY : PADY + cy, :] = jnp.where(me_x == 0, 0.0, before)
            pad_ref[plane, cx + 1, PADY : PADY + cy, :] = jnp.where(me_x == nx - 1, 0.0, after)
        if with_y:
            e, o = ye_ref[n], yo_ref[n]
            before = jnp.where(me_y == 0, 0.0, jnp.where(par_y == 0, o, e))
            after = jnp.where(me_y == ny - 1, 0.0, jnp.where(par_y == 0, e, o))
            for i in range(cx):
                pad_ref[plane, i + 1, PADY - 1 : PADY, :] = before[i : i + 1]
                pad_ref[plane, i + 1, PADY + cy : PADY + cy + 1, :] = after[i : i + 1]

    def fill_pads(pad_ref, vel_ref, dif_ref, con_ref=None):
        pad_ref[0, 1 : cx + 1, PADY : PADY + cy, :] = vel_ref[0].astype(F32)
        pad_ref[1, 1 : cx + 1, PADY : PADY + cy, :] = vel_ref[1].astype(F32)
        pad_ref[2, 1 : cx + 1, PADY : PADY + cy, :] = dif_ref[...].astype(F32)
        if con_ref is not None:
            pad_ref[3, 1 : cx + 1, PADY : PADY + cy, :] = con_ref[...].astype(F32)

    def cell_coefficients(i, jv, uz, pad_ref, fluid_ref):
        lane = lax.broadcasted_iota(jnp.int32, (8, 128), 1)
        top = lane == 127
        bottom = lane == 0

        def up(x):
            return jnp.where(top, 0.0, pltpu.roll(x, 127, axis=1))

        def down(x):
            return jnp.where(bottom, 0.0, pltpu.roll(x, 1, axis=1))

        j = PADY + 8 * jv
        at = pl.ds(i * cy + 8 * jv, 8)
        fluid = (lane.astype(F32) >= fluid_ref[at, :]).astype(F32)
        e = 0.05 * fluid
        k0 = pad_ref[2, i + 1, j : j + 8, :]
        ends = None
        out = [None]
        for plane, sign, a, b in (
            (0, 1.0, i + 2, j), (0, -1.0, i, j), (1, 1.0, i + 1, j + 1), (1, -1.0, i + 1, j - 1),
        ):
            kn = k0 + pad_ref[2, a, b : b + 8, :]
            un = pad_ref[plane, a, b : b + 8, :]
            out.append(e * (kn + un if sign > 0 else kn - un))
            ends = kn if ends is None else ends + kn
        kn = k0 + up(k0)
        ends = ends + kn
        out.append(jnp.where(top, 0.0, e * (kn + up(uz))))
        kn = k0 + down(k0)
        ends = ends + kn
        out.append(jnp.where(bottom, 0.0, e * (kn - down(uz))))
        out[0] = fluid - e * ends
        return out, e

    def cell_gradients(i, jv, e, pad_ref):
        lane = lax.broadcasted_iota(jnp.int32, (8, 128), 1)
        j = PADY + 8 * jv
        c0 = pad_ref[3, i + 1, j : j + 8, :]
        above = jnp.where(lane == 127, 0.0, pltpu.roll(c0, 127, axis=1))
        below = jnp.where(lane == 0, 0.0, pltpu.roll(c0, 1, axis=1))
        return [
            e * (pad_ref[3, i + 2, j : j + 8, :] - pad_ref[3, i, j : j + 8, :]),
            e * (pad_ref[3, i + 1, j + 1 : j + 9, :] - pad_ref[3, i + 1, j - 1 : j + 7, :]),
            e * (above - below),
        ]

    def cells():
        return [(i, jv) for i in range(cx) for jv in range(cy // 8)]

    def vertical(vel_ref, i, jv):
        pair = vel_ref[2, i, 16 * (jv // 2) : 16 * (jv // 2) + 16, :].astype(F32)
        return pair[8 * (jv % 2) : 8 * (jv % 2) + 8]

    def cell_step(i, jv, c, state_ref, k):
        j = PADY + 8 * jv
        f = state_ref[k, i + 1, j : j + 8, :]
        value = c[0] * f
        value = value + c[1] * state_ref[k, i + 2, j : j + 8, :]
        value = value + c[2] * state_ref[k, i, j : j + 8, :]
        value = value + c[3] * state_ref[k, i + 1, j + 1 : j + 9, :]
        value = value + c[4] * state_ref[k, i + 1, j - 1 : j + 7, :]
        value = value + c[5] * pltpu.roll(f, 127, axis=1)
        value = value + c[6] * pltpu.roll(f, 1, axis=1)
        return value

    def edge_row(ref, k, row):
        return ref[k, pl.ds(pl.multiple_of(row * cy, 8), cy), :]

    def edge_col(ref, k, col):
        return ref[k, pl.ds(col, cx, stride=cy), :]

    def first(
        adj_hbm, vel_hbm, dif_hbm, con_hbm, rec_hbm,
        xe_ref, xo_ref, ye_ref, yo_ref,
        adj_ref, vel_ref, dif_ref, con_ref, rec_ref, side_ref, sem,
    ):
        copies = [
            pltpu.make_async_copy(rec_hbm, rec_ref, sem.at[0]),
            pltpu.make_async_copy(vel_hbm.at[pl.ds(0, 2)], vel_ref, sem.at[1]),
            pltpu.make_async_copy(dif_hbm, dif_ref, sem.at[2]),
            pltpu.make_async_copy(con_hbm, con_ref, sem.at[3]),
            pltpu.make_async_copy(adj_hbm, adj_ref, sem.at[4]),
        ]
        start_all(copies)
        row_e, row_o, col_e, col_o = edges_at()
        copies[0].wait()
        counts = receptor_counts(rec_ref[...], cols)
        wait_all(copies[1:4])
        side_ref[0] = vel_ref[1].astype(F32).reshape(cols, 128)
        side_ref[1] = dif_ref[...].astype(F32).reshape(cols, 128)
        side_ref[2] = con_ref[...].astype(F32).reshape(cols, 128)
        for row, out in ((row_e, xe_ref), (row_o, xo_ref)):
            out[4] = vel_ref[0, row].astype(F32)
            out[5] = dif_ref[row].astype(F32)
            out[6] = con_ref[row].astype(F32)
        for col, out in ((col_e, ye_ref), (col_o, yo_ref)):
            for k in range(3):
                out[4 + k] = edge_col(side_ref, k, col)
        copies[4].wait()
        adj_ref[3] += counts
        for k in range(4):
            xe_ref[k] = edge_row(adj_ref, k, row_e)
            xo_ref[k] = edge_row(adj_ref, k, row_o)
            ye_ref[k] = edge_col(adj_ref, k, col_e)
            yo_ref[k] = edge_col(adj_ref, k, col_o)

    def second(
        adj_hbm, vel_hbm, dif_hbm, rec_hbm, height_hbm, src_hbm, weight_hbm,
        now_ref, soon_ref, hot_ref, weight_ref, exe_ref, exo_ref, eye_ref, eyo_ref,
        state_ref, vel_ref, dif_ref, rec_ref, height_ref, src_ref,
        pad_ref, fluid_ref, count_ref, next_ref, sem,
    ):
        copies = [
            pltpu.make_async_copy(src_hbm, src_ref, sem.at[0]),
            pltpu.make_async_copy(height_hbm, height_ref, sem.at[1]),
            pltpu.make_async_copy(rec_hbm, rec_ref, sem.at[2]),
            pltpu.make_async_copy(dif_hbm, dif_ref, sem.at[3]),
            pltpu.make_async_copy(
                adj_hbm.at[3], state_ref.at[0, inside[0], inside[1], :], sem.at[4]
            ),
            pltpu.make_async_copy(vel_hbm, vel_ref, sem.at[5]),
            pltpu.make_async_copy(weight_hbm, weight_ref, sem.at[6]),
        ]
        start_all(copies)
        row_e, row_o, col_e, col_o = edges_at()
        clear_halo(pad_ref, range(3))
        clear_halo(state_ref, range(1))
        copies[0].wait()
        index = row_values(src_ref[...]).astype(jnp.int32)
        copies[1].wait()
        fluid_ref[...] = row_values(height_ref[...])
        copies[2].wait()
        count_ref[...] = receptor_counts(rec_ref[...], cols)
        wait_all(copies[3:6])
        fill_pads(pad_ref, vel_ref, dif_ref)
        state_ref[0, 1 : cx + 1, PADY : PADY + cy, :] += count_ref[...].reshape(cx, cy, 128)
        for i, jv in cells():
            at = pl.ds(i * cy + 8 * jv, 8)
            c, e = cell_coefficients(i, jv, vertical(vel_ref, i, jv), pad_ref, fluid_ref)
            fluid_ref[at, :] = e
            next_ref[at, :] = cell_step(i, jv, c, state_ref, 0) + count_ref[at, :]
        lane = lax.broadcasted_iota(jnp.int32, index.shape, 1)
        i, j = index // cy, index % cy
        near = jnp.logical_or(
            jnp.logical_or(
                jnp.logical_and(i == row_e, j == lane),
                jnp.logical_and(i == row_o, j + cy == lane),
            ),
            jnp.logical_or(
                jnp.logical_and(j == col_e, i + 2 * cy == lane),
                jnp.logical_and(j == col_o, i + 2 * cy + cx == lane),
            ),
        )
        hot_ref[...] = jnp.where(jnp.logical_and(near, index >= 0), 1.0, 0.0).astype(BF16)
        hot = [(index == lane + t).astype(F32).astype(BF16) for t in range(0, cols, 128)]
        hot = jnp.concatenate(hot, axis=1)
        copies[6].wait()
        weight = weight_ref[...]
        conc = state_ref[0, 1 : cx + 1, PADY : PADY + cy, :].reshape(cols, 128)
        both = jnp.concatenate([split3(conc), split3(next_ref[...])], axis=1)
        picked = jnp.dot(hot, both, preferred_element_type=F32)
        now_ref[...] = weight * join3(picked[:, :384])
        soon_ref[...] = weight * join3(picked[:, 384:])
        exe_ref[...] = fluid_ref[pl.ds(pl.multiple_of(row_e * cy, 8), cy), :]
        exo_ref[...] = fluid_ref[pl.ds(pl.multiple_of(row_o * cy, 8), cy), :]
        eye_ref[...] = fluid_ref[pl.ds(col_e, cx, stride=cy), :]
        eyo_ref[...] = fluid_ref[pl.ds(col_o, cx, stride=cy), :]

    def edge_signs():
        me_x, me_y = lax.axis_index("gx"), lax.axis_index("gy")
        sx = (1 - 2 * lax.rem(me_x, 2)).astype(F32)
        sy = (1 - 2 * lax.rem(me_y, 2)).astype(F32)
        wrap_x = jnp.logical_or(me_x == 0, me_x == nx - 1)
        wrap_y = jnp.logical_or(me_y == 0, me_y == ny - 1)
        return sx, sy, wrap_x, wrap_y

    def edge_terms(own, halo, e, sign, wrap):
        e = e[...]
        if wrap is not None:
            e = jnp.where(wrap, 0.0, e)
        there = halo[5]
        return e * ((own[5] + there + sign * halo[4]) * halo[3] - there * own[3])

    def third(
        hxe, hxo, hyo, hye, oxe, oxo, oye, oyo, exe, exo, eye, eyo,
        now_ref, soon_ref, hot_ref, weight_ref, blocks_ref,
    ):
        sx, sy, wrap_x, wrap_y = edge_signs()
        edges = [
            edge_terms(oxe, hxe, exe, sx, None),
            edge_terms(oxo, hxo, exo, -sx, wrap_x),
            edge_terms(oye, hye, eye, sy, None),
            edge_terms(oyo, hyo, eyo, -sy, wrap_y),
        ]
        used = 2 * (cx + cy)
        edges = jnp.concatenate(edges + [jnp.zeros((128 - used, 128), F32)], axis=0)
        more = join3(jnp.dot(hot_ref[...], split3(edges), preferred_element_type=F32))
        blocks_ref[:, 0:cap, :] = now_ref[...].reshape(owners, cap, 128)
        soon = soon_ref[...] + weight_ref[...] * more
        blocks_ref[:, cap : 2 * cap, :] = soon.reshape(owners, cap, 128)

    def fourth(
        adj_hbm, vel_hbm, dif_hbm, con_hbm, rec_hbm, height_hbm, dst_hbm, hxe, hxo, hyo, hye,
        last_hbm, coef_hbm, hot_ref, xe_ref, xo_ref, ye_ref, yo_ref,
        cxe_ref, cxo_ref, cye_ref, cyo_ref,
        state_ref, vel_ref, dif_ref, con_ref, rec_ref, height_ref, dst_ref,
        pad_ref, fluid_ref, count_ref, coef_ref, next_ref, flat_ref, last_ref, sem,
    ):
        copies = [
            pltpu.make_async_copy(height_hbm, height_ref, sem.at[0]),
            pltpu.make_async_copy(vel_hbm, vel_ref, sem.at[1]),
            pltpu.make_async_copy(dif_hbm, dif_ref, sem.at[2]),
            pltpu.make_async_copy(con_hbm, con_ref, sem.at[3]),
            pltpu.make_async_copy(dst_hbm, dst_ref, sem.at[4]),
            pltpu.make_async_copy(rec_hbm, rec_ref, sem.at[5]),
            pltpu.make_async_copy(adj_hbm, state_ref.at[:, inside[0], inside[1], :], sem.at[6]),
        ]
        start_all(copies)
        row_e, row_o, col_e, col_o = edges_at()
        clear_halo(next_ref, range(4))
        halo = (hxe, hxo, hye, hyo)
        take_halo(pad_ref, 0, 4, *halo, True, False)
        take_halo(pad_ref, 1, 4, *halo, False, True)
        take_halo(pad_ref, 2, 5, *halo, True, True)
        take_halo(pad_ref, 3, 6, *halo, True, True)
        for k in range(4):
            take_halo(state_ref, k, k, *halo, True, True)
        copies[0].wait()
        fluid_ref[...] = row_values(height_ref[...])
        wait_all(copies[1:4])
        fill_pads(pad_ref, vel_ref, dif_ref, con_ref)
        wait_all(copies[4:7])
        hot_ref[...] = select_cols(dst_ref[...], cols)
        count_ref[...] = receptor_counts(rec_ref[...], cols)
        state_ref[3, 1 : cx + 1, PADY : PADY + cy, :] += count_ref[...].reshape(cx, cy, 128)
        for i, jv in cells():
            at = pl.ds(i * cy + 8 * jv, 8)
            j = PADY + 8 * jv
            c, e = cell_coefficients(i, jv, vertical(vel_ref, i, jv), pad_ref, fluid_ref)
            c = c + cell_gradients(i, jv, e, pad_ref)
            for n in range(10):
                coef_ref[n, at, :] = c[n]
            conc = state_ref[3, i + 1, j : j + 8, :]
            for k in range(4):
                value = cell_step(i, jv, c, state_ref, k)
                value = value + count_ref[at, :] if k == 3 else value - c[7 + k] * conc
                next_ref[k, i + 1, j : j + 8, :] = value
                flat_ref[k, at, :] = value
        outs = [pltpu.make_async_copy(coef_ref.at[pl.ds(0, 7)], coef_hbm, sem.at[7])]
        outs[0].start()
        for k in range(4):
            xe_ref[k] = edge_row(flat_ref, k, row_e)
            xo_ref[k] = edge_row(flat_ref, k, row_o)
            ye_ref[k] = edge_col(flat_ref, k, col_e)
            yo_ref[k] = edge_col(flat_ref, k, col_o)
        for i, jv in cells():
            at = pl.ds(i * cy + 8 * jv, 8)
            j = PADY + 8 * jv
            c = [coef_ref[n, at, :] for n in range(10)]
            conc = next_ref[3, i + 1, j : j + 8, :]
            for k in range(4):
                value = cell_step(i, jv, c, next_ref, k)
                if k < 3:
                    value = value - c[7 + k] * conc
                last_ref[k, i, 8 * jv : 8 * jv + 8, :] = value
        outs.append(pltpu.make_async_copy(last_ref, last_hbm, sem.at[8]))
        outs[1].start()
        par_x = lax.rem(lax.axis_index("gx"), 2)
        par_y = lax.rem(lax.axis_index("gy"), 2)
        cxe_ref[...] = coef_ref[1 + par_x, pl.ds(pl.multiple_of(row_e * cy, 8), cy), :]
        cxo_ref[...] = coef_ref[2 - par_x, pl.ds(pl.multiple_of(row_o * cy, 8), cy), :]
        cye_ref[...] = edge_col(coef_ref, 3 + par_y, col_e)
        cyo_ref[...] = edge_col(coef_ref, 4 - par_y, col_o)
        wait_all(outs)

    def fifth(
        arrived_ref, hot_ref, xe_in, xo_in, ye_in, yo_in,
        wall_ref, xe_ref, xo_ref, ye_ref, yo_ref,
    ):
        row_e, row_o, col_e, col_o = edges_at()
        blocks = split3(arrived_ref[:, 0:cap, :].reshape(slots, 128))
        wall_ref[0] = join3(jnp.dot(hot_ref[...], blocks, preferred_element_type=F32))
        xe_ref[...] = xe_in[...]
        xo_ref[...] = xo_in[...]
        ye_ref[...] = ye_in[...]
        yo_ref[...] = yo_in[...]
        xe_ref[2] += edge_row(wall_ref, 0, row_e)
        xo_ref[2] += edge_row(wall_ref, 0, row_o)
        ye_ref[2] += edge_col(wall_ref, 0, col_e)
        yo_ref[2] += edge_col(wall_ref, 0, col_o)

    def sixth(
        last_hbm, coef_hbm, wall_ref, arrived_ref, hot_ref,
        out_hbm, sxe_ref, sxo_ref, sye_ref, syo_ref,
        coef_ref, pad_ref, final_ref, add_ref, sem,
    ):
        row_e, row_o, col_e, col_o = edges_at()
        tile_e = pl.ds(pl.multiple_of(col_e // 8 * 8, 8), 8)
        tile_o = pl.ds(pl.multiple_of(col_o // 8 * 8, 8), 8)
        copies = [
            pltpu.make_async_copy(last_hbm.at[2], final_ref, sem.at[0]),
            pltpu.make_async_copy(coef_hbm, coef_ref, sem.at[1]),
            pltpu.make_async_copy(last_hbm.at[:, row_e], sxe_ref, sem.at[2]),
            pltpu.make_async_copy(last_hbm.at[:, row_o], sxo_ref, sem.at[3]),
            pltpu.make_async_copy(last_hbm.at[:, :, tile_e, :], sye_ref, sem.at[4]),
            pltpu.make_async_copy(last_hbm.at[:, :, tile_o, :], syo_ref, sem.at[5]),
        ]
        start_all(copies)
        blocks = split3(arrived_ref[:, cap : 2 * cap, :].reshape(slots, 128))
        add_ref[...] = join3(jnp.dot(hot_ref[...], blocks, preferred_element_type=F32))
        clear_halo(pad_ref, (0,))
        pad_ref[0, 1 : cx + 1, PADY : PADY + cy, :] = wall_ref[0].reshape(cx, cy, 128)
        wait_all(copies)
        for i, jv in cells():
            at = pl.ds(i * cy + 8 * jv, 8)
            c = [coef_ref[n, at, :] for n in range(7)]
            value = final_ref[i, 8 * jv : 8 * jv + 8, :] + add_ref[at, :]
            final_ref[i, 8 * jv : 8 * jv + 8, :] = value + cell_step(i, jv, c, pad_ref, 0)
        copy = pltpu.make_async_copy(final_ref, out_hbm.at[2], sem.at[6])
        copy.start()
        sxe_ref[2] = final_ref[row_e]
        sxo_ref[2] = final_ref[row_o]
        sye_ref[2] = final_ref[:, tile_e, :]
        syo_ref[2] = final_ref[:, tile_o, :]
        copy.wait()

    def seventh(
        last_hbm, sxe, sxo, sye, syo, hxe, hxo, hyo, hye, cxe, cxo, cye, cyo,
        out_hbm, txe, txo, tye, tyo, dye, dyo, sem,
    ):
        row_e, row_o, col_e, col_o = edges_at()
        _, _, wrap_x, wrap_y = edge_signs()
        near_e, near_o = cye[...], jnp.where(wrap_y, 0.0, cyo[...])
        tile_e = col_e // 8 * 8
        tile_o = col_o // 8 * 8
        for k in range(4):
            dye[k] = near_e * hye[k]
            dyo[k] = near_o * hyo[k]
            tye[k] = sye[k]
            tyo[k] = syo[k]
            for i in range(1, cx - 1):
                tye[k, i, pl.ds(col_e - tile_e, 1), :] += dye[k, i : i + 1, :]
                tyo[k, i, pl.ds(col_o - tile_o, 1), :] += dyo[k, i : i + 1, :]
        copies = [
            pltpu.make_async_copy(
                strip.at[:, pl.ds(1, cx - 2)],
                out_hbm.at[:, pl.ds(1, cx - 2), pl.ds(pl.multiple_of(tile, 8), 8), :],
                sem.at[n],
            )
            for n, (strip, tile) in enumerate(((tye, tile_e), (tyo, tile_o)))
        ]
        start_all(copies)
        near_e, near_o = cxe[...], jnp.where(wrap_x, 0.0, cxo[...])
        for k in range(4):
            txe[k] = sxe[k] + near_e * hxe[k]
            txo[k] = sxo[k] + near_o * hxo[k]
            for row, out in ((row_e, txe), (row_o, txo)):
                for col, dy in ((col_e, dye), (col_o, dyo)):
                    out[k, pl.ds(col, 1), :] += dy[k, pl.ds(row, 1), :]
        more = [
            pltpu.make_async_copy(strip, out_hbm.at[:, row], sem.at[n])
            for n, (strip, row) in enumerate(((txe, row_e), (txo, row_o)), 2)
        ]
        start_all(more)
        wait_all(copies + more)

    def sds(*shape):
        return jax.ShapeDtypeStruct(shape, F32)

    def hbm(*shape):
        return pltpu.HBM(shape, F32)

    def vm(*shape, dtype=F32):
        return pltpu.VMEM(shape, dtype)

    def dma(count):
        return pltpu.SemaphoreType.DMA((count,))

    def call(body, name, ins, outs, shapes, scratch, cost, limit=24, **more):
        return pl.pallas_call(
            body,
            name=name,
            out_shape=shapes,
            in_specs=ins,
            out_specs=outs,
            scratch_shapes=scratch,
            compiler_params=pltpu.CompilerParams(vmem_limit_bytes=limit << 20),
            cost_estimate=pl.CostEstimate(flops=cost, bytes_accessed=cost, transcendentals=0),
            **more,
        )

    int_table = vm(owners, cap, dtype=jnp.int32)
    three = [vm(3, cx, cy, 128, dtype=BF16)] + [vm(cx, cy, 128, dtype=BF16)] * 2
    strips = (sds(4, cy, 128), sds(4, cy, 128), sds(4, cx, 128), sds(4, cx, 128))
    sides = (sds(cy, 128), sds(cy, 128), sds(cx, 128), sds(cx, 128))
    height = vm(cx, cy, dtype=jnp.int32)
    padded = vm(4, px, py, 128)

    def kernels(rcp):
        line = vm(1, rcp, dtype=jnp.int32)
        return (
            call(
                first, "first", [HBM] * 5, (VMEM,) * 4,
                (sds(7, cy, 128), sds(7, cy, 128), sds(7, cx, 128), sds(7, cx, 128)),
                [vm(4, cols, 128), vm(2, cx, cy, 128, dtype=BF16)] + three[1:]
                + [line, vm(3, cols, 128), dma(5)],
                4 << 20,
            ),
            call(
                second, "second", [HBM] * 7, (VMEM,) * 8,
                (sds(slots, 128), sds(slots, 128),
                 jax.ShapeDtypeStruct((slots, 128), BF16), sds(slots, 128)) + sides,
                [vm(1, px, py, 128)] + three[:2] + [line, height, int_table]
                + [vm(3, px, py, 128), vm(cols, 128), vm(cols, 128), vm(cols, 128), dma(7)],
                8 << 20,
            ),
            call(
                third, "third", [VMEM] * 16, VMEM, sds(owners, 2 * cap, 128), [], 2 << 20,
            ),
            call(
                fourth, "fourth", [HBM] * 7 + [VMEM] * 4, (HBM,) * 2 + (VMEM,) * 9,
                (hbm(4, cx, cy, 128), hbm(7, cols, 128), jax.ShapeDtypeStruct((cols, slots), BF16))
                + strips + sides,
                [padded] + three + [line, height, int_table]
                + [padded, vm(cols, 128), vm(cols, 128), vm(10, cols, 128), padded,
                   vm(4, cols, 128), vm(4, cx, cy, 128), dma(9)],
                10 << 20,
            ),
            call(
                fifth, "fifth", [VMEM] * 6, (VMEM,) * 5, (sds(1, cols, 128),) + strips, [],
                2 << 20,
            ),
            call(
                sixth, "sixth", [HBM] * 2 + [VMEM] * 3, (HBM,) + (VMEM,) * 4,
                (hbm(4, cx, cy, 128), sds(4, cy, 128), sds(4, cy, 128),
                 sds(4, cx, 8, 128), sds(4, cx, 8, 128)),
                [vm(7, cols, 128), vm(1, px, py, 128), vm(cx, cy, 128), vm(cols, 128), dma(7)],
                5 << 20,
                input_output_aliases={0: 0},
            ),
            call(
                seventh, "seventh", [HBM] + [VMEM] * 12, HBM, sds(4, cx, cy, 128),
                [vm(4, cy, 128), vm(4, cy, 128), vm(4, cx, 8, 128), vm(4, cx, 8, 128),
                 vm(4, cx, 128), vm(4, cx, 128), dma(4)],
                2 << 20,
                input_output_aliases={0: 0},
            ),
        )

    return kernels


def shards(
    adjoint, velocity, diffusivity, concentration, heights, receptors, face_src, face_dst, face_coef
):
    nx, ny = lax.axis_size("gx"), lax.axis_size("gy")
    cx, cy, levels = adjoint.shape[1:]
    owners, cap = face_src.shape[2:]
    kernels = make_kernels(nx, ny, cx, cy, owners, cap)
    first, second, third, fourth, fifth, sixth, seventh = kernels(receptors.shape[2])

    def swap(partner):
        return [
            (x * ny + y, px * ny + py)
            for x in range(nx) for y in range(ny) for px, py in (partner(x, y),)
        ]

    def odd(i):
        return i - 1 if i % 2 == 0 else i + 1

    x_even = swap(lambda x, y: (x ^ 1, y))
    x_odd = swap(lambda x, y: (odd(x), y) if 0 < x < nx - 1 else (x, y ^ 1))
    y_even = swap(lambda x, y: (x, y ^ 1))
    y_odd = swap(lambda x, y: (x, odd(y)) if 0 < y < ny - 1 else (x ^ 1, y))

    def exchange(*edges):
        swaps = (x_even, x_odd, y_even, y_odd)
        return [lax.ppermute(e, ("gx", "gy"), pairs) for e, pairs in zip(edges, swaps)]

    src = face_src.reshape(owners, cap)
    dst = face_dst.reshape(owners, cap)
    weight = face_coef.reshape(owners * cap, levels)
    line = receptors.reshape(1, -1)
    flat = adjoint.reshape(4, cx * cy, levels)

    def pinned(*arrays):
        return [pltpu.with_memory_space_constraint(x, pltpu.HBM) for x in arrays]

    own = first(*pinned(flat, velocity, diffusivity, concentration, line))
    halos = exchange(*own)
    now, soon, hot, weight, *fluid = second(
        *pinned(adjoint, velocity, diffusivity, line, heights, src, weight)
    )
    blocks = third(*[halos[n] for n in [0, 1, 3, 2]], *own, *fluid, now, soon, hot, weight)
    arrived = lax.all_to_all(blocks, "gx", split_axis=0, concat_axis=0, tiled=True)
    last, coefs, hot, *rest = fourth(
        *pinned(adjoint, velocity, diffusivity, concentration, line, heights, dst), *[halos[n] for n in [0, 1, 3, 2]]
    )
    edges, sides = rest[:4], rest[4:]
    wall, *edges = fifth(arrived, hot, *edges)
    halos = exchange(*edges)
    out, *strips = sixth(*pinned(last, coefs), wall, arrived, hot)
    return seventh(*pinned(out), *strips, *[halos[n] for n in [0, 1, 3, 2]], *sides)


def solution(mesh):
    placed = (
        P(None, "gx", "gy", None),
        P(None, "gx", "gy", None),
        P("gx", "gy", None),
        P("gx", "gy", None),
        P("gx", "gy"),
        P("gx", "gy", None),
        P("gx", "gy", None, None),
        P("gx", "gy", None, None),
        P("gx", "gy", None, None, None),
    )
    return jax.shard_map(
        shards, mesh=mesh, in_specs=placed, out_specs=P(None, "gx", "gy", None), check_vma=False
    )
```

```python
import jax
import jax.numpy as jnp
from jax import lax
from jax.experimental import pallas as pl
from jax.experimental.pallas import tpu as pltpu
from jax.sharding import PartitionSpec as P

F32 = jnp.float32
BF16 = jnp.bfloat16
PADY = 8
VMEM = pl.BlockSpec(memory_space=pltpu.VMEM)
HBM = pl.BlockSpec(memory_space=pltpu.HBM)


def split3(x):
    hi = x.astype(BF16)
    rest = x - hi.astype(F32)
    mid = rest.astype(BF16)
    low = (rest - mid.astype(F32)).astype(BF16)
    return jnp.concatenate([hi, mid, low], axis=1)


def join3(x):
    return x[:, :128] + x[:, 128:256] + x[:, 256:384]


def row_values(table):
    n = table.shape[1]
    eye = lax.broadcasted_iota(jnp.int32, (n, n), 0) == lax.broadcasted_iota(jnp.int32, (n, n), 1)
    high = table >> 4
    low = table & 15
    ones = jnp.ones((n, 128), BF16)
    total = None
    for part in (high * 16, low):
        part = part.astype(F32)
        rows = [
            jnp.where(eye, jnp.broadcast_to(part[d : d + 1], (n, n)), 0.0)
            for d in range(table.shape[0])
        ]
        spread = jnp.concatenate(rows, axis=0).astype(BF16)
        value = jnp.dot(spread, ones, preferred_element_type=F32)
        total = value if total is None else total + value
    return total


def select_cols(table, cols):
    d_count, n = table.shape
    slots = d_count * n
    tile = (
        lax.broadcasted_iota(jnp.int32, (n, slots), 1) % n
        == lax.broadcasted_iota(jnp.int32, (n, slots), 0)
    ).astype(F32).astype(BF16)
    mine = (
        lax.broadcasted_iota(jnp.int32, (d_count, slots), 1) // n
        == lax.broadcasted_iota(jnp.int32, (d_count, slots), 0)
    )
    high = ((table >> 4) * 16).astype(F32).astype(BF16)
    low = (table & 15).astype(F32).astype(BF16)
    value = jnp.dot(high, tile, preferred_element_type=F32) + jnp.dot(
        low, tile, preferred_element_type=F32
    )
    line = jnp.sum(jnp.where(mine, value, 0.0), axis=0, keepdims=True).astype(jnp.int32)
    col = lax.broadcasted_iota(jnp.int32, (cols, slots), 0)
    return (col == line).astype(F32).astype(BF16)


def receptor_counts(line, cols):
    entries = line.shape[1]
    col = lax.broadcasted_iota(jnp.int32, (cols, entries), 0)
    level = lax.broadcasted_iota(jnp.int32, (128, entries), 0)
    hot_col = (col == (line >> 7)).astype(F32).astype(BF16)
    hot_level = (level == (line & 127)).astype(F32).astype(BF16)
    return lax.dot_general(
        hot_col, hot_level, (((1,), (1,)), ((), ())), preferred_element_type=F32
    )


def make_kernels(nx, ny, cx, cy, owners, cap):
    cols = cx * cy
    slots = owners * cap
    px, py = cx + 2, cy + 2 * PADY
    inside = (pl.ds(1, cx), pl.ds(PADY, cy))

    def edges_at():
        par_x = lax.rem(lax.axis_index("gx"), 2)
        par_y = lax.rem(lax.axis_index("gy"), 2)
        return (
            (cx - 1) * (1 - par_x), (cx - 1) * par_x,
            (cy - 1) * (1 - par_y), (cy - 1) * par_y,
        )

    def start_all(copies):
        for copy in copies:
            copy.start()

    def wait_all(copies):
        for copy in copies:
            copy.wait()

    def clear_halo(pad_ref, planes):
        zero = jnp.zeros((px, PADY, 128), F32)
        row = jnp.zeros((cy, 128), F32)
        for k in planes:
            pad_ref[k, :, 0:PADY, :] = zero
            pad_ref[k, :, PADY + cy : py, :] = zero
            pad_ref[k, 0, PADY : PADY + cy, :] = row
            pad_ref[k, cx + 1, PADY : PADY + cy, :] = row

    def take_halo(pad_ref, plane, n, xe_ref, xo_ref, ye_ref, yo_ref, with_x, with_y):
        me_x, me_y = lax.axis_index("gx"), lax.axis_index("gy")
        par_x, par_y = lax.rem(me_x, 2), lax.rem(me_y, 2)
        if with_x:
            e, o = xe_ref[n], xo_ref[n]
            before = jnp.where(par_x == 0, o, e)
            after = jnp.where(par_x == 0, e, o)
            pad_ref[plane, 0, PADY : PADY + cy, :] = jnp.where(me_x == 0, 0.0, before)
            pad_ref[plane, cx + 1, PADY : PADY + cy, :] = jnp.where(me_x == nx - 1, 0.0, after)
        if with_y:
            e, o = ye_ref[n], yo_ref[n]
            before = jnp.where(me_y == 0, 0.0, jnp.where(par_y == 0, o, e))
            after = jnp.where(me_y == ny - 1, 0.0, jnp.where(par_y == 0, e, o))
            for i in range(cx):
                pad_ref[plane, i + 1, PADY - 1 : PADY, :] = before[i : i + 1]
                pad_ref[plane, i + 1, PADY + cy : PADY + cy + 1, :] = after[i : i + 1]

    def fill_pads(pad_ref, vel_ref, dif_ref, con_ref=None):
        pad_ref[0, 1 : cx + 1, PADY : PADY + cy, :] = vel_ref[0].astype(F32)
        pad_ref[1, 1 : cx + 1, PADY : PADY + cy, :] = vel_ref[1].astype(F32)
        pad_ref[2, 1 : cx + 1, PADY : PADY + cy, :] = dif_ref[...].astype(F32)
        if con_ref is not None:
            pad_ref[3, 1 : cx + 1, PADY : PADY + cy, :] = con_ref[...].astype(F32)

    def cell_coefficients(i, jv, uz, pad_ref, fluid_ref):
        lane = lax.broadcasted_iota(jnp.int32, (8, 128), 1)
        top = lane == 127
        bottom = lane == 0

        def up(x):
            return jnp.where(top, 0.0, pltpu.roll(x, 127, axis=1))

        def down(x):
            return jnp.where(bottom, 0.0, pltpu.roll(x, 1, axis=1))

        j = PADY + 8 * jv
        at = pl.ds(i * cy + 8 * jv, 8)
        fluid = (lane.astype(F32) >= fluid_ref[at, :]).astype(F32)
        e = 0.05 * fluid
        k0 = pad_ref[2, i + 1, j : j + 8, :]
        ends = None
        out = [None]
        for plane, sign, a, b in (
            (0, 1.0, i + 2, j), (0, -1.0, i, j), (1, 1.0, i + 1, j + 1), (1, -1.0, i + 1, j - 1),
        ):
            kn = k0 + pad_ref[2, a, b : b + 8, :]
            un = pad_ref[plane, a, b : b + 8, :]
            out.append(e * (kn + un if sign > 0 else kn - un))
            ends = kn if ends is None else ends + kn
        kn = k0 + up(k0)
        ends = ends + kn
        out.append(jnp.where(top, 0.0, e * (kn + up(uz))))
        kn = k0 + down(k0)
        ends = ends + kn
        out.append(jnp.where(bottom, 0.0, e * (kn - down(uz))))
        out[0] = fluid - e * ends
        return out, e

    def cell_gradients(i, jv, e, pad_ref):
        lane = lax.broadcasted_iota(jnp.int32, (8, 128), 1)
        j = PADY + 8 * jv
        c0 = pad_ref[3, i + 1, j : j + 8, :]
        above = jnp.where(lane == 127, 0.0, pltpu.roll(c0, 127, axis=1))
        below = jnp.where(lane == 0, 0.0, pltpu.roll(c0, 1, axis=1))
        return [
            e * (pad_ref[3, i + 2, j : j + 8, :] - pad_ref[3, i, j : j + 8, :]),
            e * (pad_ref[3, i + 1, j + 1 : j + 9, :] - pad_ref[3, i + 1, j - 1 : j + 7, :]),
            e * (above - below),
        ]

    def cells():
        return [(i, jv) for i in range(cx) for jv in range(cy // 8)]

    def vertical(vel_ref, i, jv):
        pair = vel_ref[2, i, 16 * (jv // 2) : 16 * (jv // 2) + 16, :].astype(F32)
        return pair[8 * (jv % 2) : 8 * (jv % 2) + 8]

    def cell_step(i, jv, c, state_ref, k):
        j = PADY + 8 * jv
        f = state_ref[k, i + 1, j : j + 8, :]
        value = c[0] * f
        value = value + c[1] * state_ref[k, i + 2, j : j + 8, :]
        value = value + c[2] * state_ref[k, i, j : j + 8, :]
        value = value + c[3] * state_ref[k, i + 1, j + 1 : j + 9, :]
        value = value + c[4] * state_ref[k, i + 1, j - 1 : j + 7, :]
        value = value + c[5] * pltpu.roll(f, 127, axis=1)
        value = value + c[6] * pltpu.roll(f, 1, axis=1)
        return value

    def edge_row(ref, k, row):
        return ref[k, pl.ds(pl.multiple_of(row * cy, 8), cy), :]

    def edge_col(ref, k, col):
        return ref[k, pl.ds(col, cx, stride=cy), :]

    def first(
        adj_hbm, vel_hbm, dif_hbm, con_hbm, rec_hbm,
        conc_ref, count_ref, xe_ref, xo_ref, ye_ref, yo_ref,
        adj_ref, vel_ref, dif_ref, con_ref, rec_ref, side_ref, sem,
    ):
        copies = [
            pltpu.make_async_copy(rec_hbm, rec_ref, sem.at[0]),
            pltpu.make_async_copy(vel_hbm.at[pl.ds(0, 2)], vel_ref, sem.at[1]),
            pltpu.make_async_copy(dif_hbm, dif_ref, sem.at[2]),
            pltpu.make_async_copy(con_hbm, con_ref, sem.at[3]),
            pltpu.make_async_copy(adj_hbm, adj_ref, sem.at[4]),
        ]
        start_all(copies)
        row_e, row_o, col_e, col_o = edges_at()
        copies[0].wait()
        counts = receptor_counts(rec_ref[...], cols)
        count_ref[...] = counts
        wait_all(copies[1:4])
        side_ref[0] = vel_ref[1].astype(F32).reshape(cols, 128)
        side_ref[1] = dif_ref[...].astype(F32).reshape(cols, 128)
        side_ref[2] = con_ref[...].astype(F32).reshape(cols, 128)
        for row, out in ((row_e, xe_ref), (row_o, xo_ref)):
            out[4] = vel_ref[0, row].astype(F32)
            out[5] = dif_ref[row].astype(F32)
            out[6] = con_ref[row].astype(F32)
        for col, out in ((col_e, ye_ref), (col_o, yo_ref)):
            for k in range(3):
                out[4 + k] = edge_col(side_ref, k, col)
        copies[4].wait()
        conc = adj_ref[3] + counts
        adj_ref[3] = conc
        conc_ref[...] = conc
        for k in range(4):
            xe_ref[k] = edge_row(adj_ref, k, row_e)
            xo_ref[k] = edge_row(adj_ref, k, row_o)
            ye_ref[k] = edge_col(adj_ref, k, col_e)
            yo_ref[k] = edge_col(adj_ref, k, col_o)

    def second(
        conc_ref, count_ref, vel_hbm, dif_hbm, height_hbm, src_hbm, weight_hbm,
        now_ref, soon_ref, hot_ref, weight_ref, exe_ref, exo_ref, eye_ref, eyo_ref,
        state_ref, vel_ref, dif_ref, height_ref, src_ref,
        pad_ref, fluid_ref, next_ref, sem,
    ):
        copies = [
            pltpu.make_async_copy(src_hbm, src_ref, sem.at[0]),
            pltpu.make_async_copy(height_hbm, height_ref, sem.at[1]),
            pltpu.make_async_copy(dif_hbm, dif_ref, sem.at[2]),
            pltpu.make_async_copy(vel_hbm, vel_ref, sem.at[3]),
            pltpu.make_async_copy(weight_hbm, weight_ref, sem.at[4]),
        ]
        start_all(copies)
        row_e, row_o, col_e, col_o = edges_at()
        clear_halo(pad_ref, range(3))
        clear_halo(state_ref, range(1))
        copies[0].wait()
        index = row_values(src_ref[...]).astype(jnp.int32)
        copies[1].wait()
        fluid_ref[...] = row_values(height_ref[...])
        state_ref[0, 1 : cx + 1, PADY : PADY + cy, :] = conc_ref[...].reshape(cx, cy, 128)
        wait_all(copies[2:4])
        fill_pads(pad_ref, vel_ref, dif_ref)
        for i, jv in cells():
            at = pl.ds(i * cy + 8 * jv, 8)
            c, e = cell_coefficients(i, jv, vertical(vel_ref, i, jv), pad_ref, fluid_ref)
            fluid_ref[at, :] = e
            next_ref[at, :] = cell_step(i, jv, c, state_ref, 0) + count_ref[at, :]
        lane = lax.broadcasted_iota(jnp.int32, index.shape, 1)
        i, j = index // cy, index % cy
        near = jnp.logical_or(
            jnp.logical_or(
                jnp.logical_and(i == row_e, j == lane),
                jnp.logical_and(i == row_o, j + cy == lane),
            ),
            jnp.logical_or(
                jnp.logical_and(j == col_e, i + 2 * cy == lane),
                jnp.logical_and(j == col_o, i + 2 * cy + cx == lane),
            ),
        )
        hot_ref[...] = jnp.where(jnp.logical_and(near, index >= 0), 1.0, 0.0).astype(BF16)
        hot = [(index == lane + t).astype(F32).astype(BF16) for t in range(0, cols, 128)]
        hot = jnp.concatenate(hot, axis=1)
        copies[4].wait()
        weight = weight_ref[...]
        conc = conc_ref[...]
        both = jnp.concatenate([split3(conc), split3(next_ref[...])], axis=1)
        picked = jnp.dot(hot, both, preferred_element_type=F32)
        now_ref[...] = weight * join3(picked[:, :384])
        soon_ref[...] = weight * join3(picked[:, 384:])
        exe_ref[...] = fluid_ref[pl.ds(pl.multiple_of(row_e * cy, 8), cy), :]
        exo_ref[...] = fluid_ref[pl.ds(pl.multiple_of(row_o * cy, 8), cy), :]
        eye_ref[...] = fluid_ref[pl.ds(col_e, cx, stride=cy), :]
        eyo_ref[...] = fluid_ref[pl.ds(col_o, cx, stride=cy), :]

    def edge_signs():
        me_x, me_y = lax.axis_index("gx"), lax.axis_index("gy")
        sx = (1 - 2 * lax.rem(me_x, 2)).astype(F32)
        sy = (1 - 2 * lax.rem(me_y, 2)).astype(F32)
        wrap_x = jnp.logical_or(me_x == 0, me_x == nx - 1)
        wrap_y = jnp.logical_or(me_y == 0, me_y == ny - 1)
        return sx, sy, wrap_x, wrap_y

    def edge_terms(own, halo, e, sign, wrap):
        e = e[...]
        if wrap is not None:
            e = jnp.where(wrap, 0.0, e)
        there = halo[5]
        return e * ((own[5] + there + sign * halo[4]) * halo[3] - there * own[3])

    def third(
        hxe, hxo, hyo, hye, oxe, oxo, oye, oyo, exe, exo, eye, eyo,
        now_ref, soon_ref, hot_ref, weight_ref, blocks_ref,
    ):
        sx, sy, wrap_x, wrap_y = edge_signs()
        edges = [
            edge_terms(oxe, hxe, exe, sx, None),
            edge_terms(oxo, hxo, exo, -sx, wrap_x),
            edge_terms(oye, hye, eye, sy, None),
            edge_terms(oyo, hyo, eyo, -sy, wrap_y),
        ]
        used = 2 * (cx + cy)
        edges = jnp.concatenate(edges + [jnp.zeros((128 - used, 128), F32)], axis=0)
        more = join3(jnp.dot(hot_ref[...], split3(edges), preferred_element_type=F32))
        blocks_ref[:, 0:cap, :] = now_ref[...].reshape(owners, cap, 128)
        soon = soon_ref[...] + weight_ref[...] * more
        blocks_ref[:, cap : 2 * cap, :] = soon.reshape(owners, cap, 128)

    def fourth(
        adj_hbm, vel_hbm, dif_hbm, con_hbm, rec_hbm, height_hbm, dst_hbm, hxe, hxo, hyo, hye,
        last_hbm, coef_out, hot_ref, xe_ref, xo_ref, ye_ref, yo_ref,
        cxe_ref, cxo_ref, cye_ref, cyo_ref,
        state_ref, vel_ref, dif_ref, con_ref, rec_ref, height_ref, dst_ref,
        pad_ref, fluid_ref, count_ref, coef_ref, next_ref, flat_ref, last_ref, sem,
    ):
        copies = [
            pltpu.make_async_copy(height_hbm, height_ref, sem.at[0]),
            pltpu.make_async_copy(vel_hbm, vel_ref, sem.at[1]),
            pltpu.make_async_copy(dif_hbm, dif_ref, sem.at[2]),
            pltpu.make_async_copy(con_hbm, con_ref, sem.at[3]),
            pltpu.make_async_copy(dst_hbm, dst_ref, sem.at[4]),
            pltpu.make_async_copy(rec_hbm, rec_ref, sem.at[5]),
            pltpu.make_async_copy(adj_hbm, state_ref.at[:, inside[0], inside[1], :], sem.at[6]),
        ]
        start_all(copies)
        row_e, row_o, col_e, col_o = edges_at()
        clear_halo(next_ref, range(4))
        halo = (hxe, hxo, hye, hyo)
        take_halo(pad_ref, 0, 4, *halo, True, False)
        take_halo(pad_ref, 1, 4, *halo, False, True)
        take_halo(pad_ref, 2, 5, *halo, True, True)
        take_halo(pad_ref, 3, 6, *halo, True, True)
        for k in range(4):
            take_halo(state_ref, k, k, *halo, True, True)
        copies[0].wait()
        fluid_ref[...] = row_values(height_ref[...])
        wait_all(copies[1:4])
        fill_pads(pad_ref, vel_ref, dif_ref, con_ref)
        wait_all(copies[4:7])
        hot_ref[...] = select_cols(dst_ref[...], cols)
        count_ref[...] = receptor_counts(rec_ref[...], cols)
        state_ref[3, 1 : cx + 1, PADY : PADY + cy, :] += count_ref[...].reshape(cx, cy, 128)
        for i, jv in cells():
            at = pl.ds(i * cy + 8 * jv, 8)
            j = PADY + 8 * jv
            c, e = cell_coefficients(i, jv, vertical(vel_ref, i, jv), pad_ref, fluid_ref)
            c = c + cell_gradients(i, jv, e, pad_ref)
            for n in range(10):
                if n < 7:
                    coef_out[n, at, :] = c[n]
                coef_ref[n, at, :] = c[n]
            conc = state_ref[3, i + 1, j : j + 8, :]
            for k in range(4):
                value = cell_step(i, jv, c, state_ref, k)
                value = value + count_ref[at, :] if k == 3 else value - c[7 + k] * conc
                next_ref[k, i + 1, j : j + 8, :] = value
                flat_ref[k, at, :] = value
        for k in range(4):
            xe_ref[k] = edge_row(flat_ref, k, row_e)
            xo_ref[k] = edge_row(flat_ref, k, row_o)
            ye_ref[k] = edge_col(flat_ref, k, col_e)
            yo_ref[k] = edge_col(flat_ref, k, col_o)
        for i, jv in cells():
            at = pl.ds(i * cy + 8 * jv, 8)
            j = PADY + 8 * jv
            c = [coef_ref[n, at, :] for n in range(10)]
            conc = next_ref[3, i + 1, j : j + 8, :]
            for k in range(4):
                value = cell_step(i, jv, c, next_ref, k)
                if k < 3:
                    value = value - c[7 + k] * conc
                last_ref[k, i, 8 * jv : 8 * jv + 8, :] = value
        out = pltpu.make_async_copy(last_ref, last_hbm, sem.at[7])
        out.start()
        par_x = lax.rem(lax.axis_index("gx"), 2)
        par_y = lax.rem(lax.axis_index("gy"), 2)
        cxe_ref[...] = coef_ref[1 + par_x, pl.ds(pl.multiple_of(row_e * cy, 8), cy), :]
        cxo_ref[...] = coef_ref[2 - par_x, pl.ds(pl.multiple_of(row_o * cy, 8), cy), :]
        cye_ref[...] = edge_col(coef_ref, 3 + par_y, col_e)
        cyo_ref[...] = edge_col(coef_ref, 4 - par_y, col_o)
        out.wait()

    def fifth(
        arrived_ref, hot_ref, xe_in, xo_in, ye_in, yo_in,
        wall_ref, xe_ref, xo_ref, ye_ref, yo_ref,
    ):
        row_e, row_o, col_e, col_o = edges_at()
        blocks = split3(arrived_ref[:, 0:cap, :].reshape(slots, 128))
        wall_ref[0] = join3(jnp.dot(hot_ref[...], blocks, preferred_element_type=F32))
        xe_ref[...] = xe_in[...]
        xo_ref[...] = xo_in[...]
        ye_ref[...] = ye_in[...]
        yo_ref[...] = yo_in[...]
        xe_ref[2] += edge_row(wall_ref, 0, row_e)
        xo_ref[2] += edge_row(wall_ref, 0, row_o)
        ye_ref[2] += edge_col(wall_ref, 0, col_e)
        yo_ref[2] += edge_col(wall_ref, 0, col_o)

    def sixth(
        last_hbm, coef_ref, wall_ref, arrived_ref, hot_ref,
        out_hbm, sxe_ref, sxo_ref, sye_ref, syo_ref,
        pad_ref, final_ref, add_ref, sem,
    ):
        row_e, row_o, col_e, col_o = edges_at()
        tile_e = pl.ds(pl.multiple_of(col_e // 8 * 8, 8), 8)
        tile_o = pl.ds(pl.multiple_of(col_o // 8 * 8, 8), 8)
        copies = [
            pltpu.make_async_copy(last_hbm.at[2], final_ref, sem.at[0]),
            pltpu.make_async_copy(last_hbm.at[:, row_e], sxe_ref, sem.at[2]),
            pltpu.make_async_copy(last_hbm.at[:, row_o], sxo_ref, sem.at[3]),
            pltpu.make_async_copy(last_hbm.at[:, :, tile_e, :], sye_ref, sem.at[4]),
            pltpu.make_async_copy(last_hbm.at[:, :, tile_o, :], syo_ref, sem.at[5]),
        ]
        start_all(copies)
        blocks = split3(arrived_ref[:, cap : 2 * cap, :].reshape(slots, 128))
        add_ref[...] = join3(jnp.dot(hot_ref[...], blocks, preferred_element_type=F32))
        clear_halo(pad_ref, (0,))
        pad_ref[0, 1 : cx + 1, PADY : PADY + cy, :] = wall_ref[0].reshape(cx, cy, 128)
        wait_all(copies)
        outs = []
        for i, jv in cells():
            at = pl.ds(i * cy + 8 * jv, 8)
            c = [coef_ref[n, at, :] for n in range(7)]
            value = final_ref[i, 8 * jv : 8 * jv + 8, :] + add_ref[at, :]
            final_ref[i, 8 * jv : 8 * jv + 8, :] = value + cell_step(i, jv, c, pad_ref, 0)
            if (i + 1) % (cx // 4) == 0 and jv == cy // 8 - 1:
                rows = pl.ds(i + 1 - cx // 4, cx // 4)
                done = len(outs)
                outs.append(
                    pltpu.make_async_copy(
                        final_ref.at[rows], out_hbm.at[2, rows], sem.at[6 + done]
                    )
                )
                outs[done].start()
        sxe_ref[2] = final_ref[row_e]
        sxo_ref[2] = final_ref[row_o]
        sye_ref[2] = final_ref[:, tile_e, :]
        syo_ref[2] = final_ref[:, tile_o, :]
        wait_all(outs)

    def seventh(
        last_hbm, sxe, sxo, sye, syo, hxe, hxo, hyo, hye, cxe, cxo, cye, cyo,
        out_hbm, txe, txo, tye, tyo, dye, dyo, sem,
    ):
        row_e, row_o, col_e, col_o = edges_at()
        _, _, wrap_x, wrap_y = edge_signs()
        near_e, near_o = cye[...], jnp.where(wrap_y, 0.0, cyo[...])
        tile_e = col_e // 8 * 8
        tile_o = col_o // 8 * 8
        for k in range(4):
            dye[k] = near_e * hye[k]
            dyo[k] = near_o * hyo[k]
            tye[k] = sye[k]
            tyo[k] = syo[k]
            for i in range(1, cx - 1):
                tye[k, i, pl.ds(col_e - tile_e, 1), :] += dye[k, i : i + 1, :]
                tyo[k, i, pl.ds(col_o - tile_o, 1), :] += dyo[k, i : i + 1, :]
        copies = [
            pltpu.make_async_copy(
                strip.at[:, pl.ds(1, cx - 2)],
                out_hbm.at[:, pl.ds(1, cx - 2), pl.ds(pl.multiple_of(tile, 8), 8), :],
                sem.at[n],
            )
            for n, (strip, tile) in enumerate(((tye, tile_e), (tyo, tile_o)))
        ]
        start_all(copies)
        near_e, near_o = cxe[...], jnp.where(wrap_x, 0.0, cxo[...])
        for k in range(4):
            txe[k] = sxe[k] + near_e * hxe[k]
            txo[k] = sxo[k] + near_o * hxo[k]
            for row, out in ((row_e, txe), (row_o, txo)):
                for col, dy in ((col_e, dye), (col_o, dyo)):
                    out[k, pl.ds(col, 1), :] += dy[k, pl.ds(row, 1), :]
        more = [
            pltpu.make_async_copy(strip, out_hbm.at[:, row], sem.at[n])
            for n, (strip, row) in enumerate(((txe, row_e), (txo, row_o)), 2)
        ]
        start_all(more)
        wait_all(copies + more)

    def sds(*shape):
        return jax.ShapeDtypeStruct(shape, F32)

    def hbm(*shape):
        return pltpu.HBM(shape, F32)

    def vm(*shape, dtype=F32):
        return pltpu.VMEM(shape, dtype)

    def dma(count):
        return pltpu.SemaphoreType.DMA((count,))

    def call(body, name, ins, outs, shapes, scratch, cost, limit=24, **more):
        return pl.pallas_call(
            body,
            name=name,
            out_shape=shapes,
            in_specs=ins,
            out_specs=outs,
            scratch_shapes=scratch,
            compiler_params=pltpu.CompilerParams(vmem_limit_bytes=limit << 20),
            cost_estimate=pl.CostEstimate(flops=cost, bytes_accessed=cost, transcendentals=0),
            **more,
        )

    int_table = vm(owners, cap, dtype=jnp.int32)
    three = [vm(3, cx, cy, 128, dtype=BF16)] + [vm(cx, cy, 128, dtype=BF16)] * 2
    strips = (sds(4, cy, 128), sds(4, cy, 128), sds(4, cx, 128), sds(4, cx, 128))
    sides = (sds(cy, 128), sds(cy, 128), sds(cx, 128), sds(cx, 128))
    height = vm(cx, cy, dtype=jnp.int32)
    padded = vm(4, px, py, 128)

    def kernels(rcp):
        line = vm(1, rcp, dtype=jnp.int32)
        return (
            call(
                first, "first", [HBM] * 5, (VMEM,) * 6,
                (sds(cols, 128), sds(cols, 128), sds(7, cy, 128), sds(7, cy, 128), sds(7, cx, 128), sds(7, cx, 128)),
                [vm(4, cols, 128), vm(2, cx, cy, 128, dtype=BF16)] + three[1:]
                + [line, vm(3, cols, 128), dma(5)],
                4 << 20,
            ),
            call(
                second, "second", [VMEM] * 2 + [HBM] * 5, (VMEM,) * 8,
                (sds(slots, 128), sds(slots, 128),
                 jax.ShapeDtypeStruct((slots, 128), BF16), sds(slots, 128)) + sides,
                [vm(1, px, py, 128)] + three[:2] + [height, int_table]
                + [vm(3, px, py, 128), vm(cols, 128), vm(cols, 128), dma(5)],
                8 << 20,
            ),
            call(
                third, "third", [VMEM] * 16, VMEM, sds(owners, 2 * cap, 128), [], 2 << 20,
            ),
            call(
                fourth, "fourth", [HBM] * 7 + [VMEM] * 4, (HBM,) + (VMEM,) * 10,
                (hbm(4, cx, cy, 128), sds(7, cols, 128), jax.ShapeDtypeStruct((cols, slots), BF16))
                + strips + sides,
                [padded] + three + [line, height, int_table]
                + [padded, vm(cols, 128), vm(cols, 128), vm(10, cols, 128), padded,
                   vm(4, cols, 128), vm(4, cx, cy, 128), dma(8)],
                10 << 20,
            ),
            call(
                fifth, "fifth", [VMEM] * 6, (VMEM,) * 5, (sds(1, cols, 128),) + strips, [],
                2 << 20,
            ),
            call(
                sixth, "sixth", [HBM] + [VMEM] * 4, (HBM,) + (VMEM,) * 4,
                (hbm(4, cx, cy, 128), sds(4, cy, 128), sds(4, cy, 128),
                 sds(4, cx, 8, 128), sds(4, cx, 8, 128)),
                [vm(1, px, py, 128), vm(cx, cy, 128), vm(cols, 128), dma(10)],
                5 << 20,
                input_output_aliases={0: 0},
            ),
            call(
                seventh, "seventh", [HBM] + [VMEM] * 12, HBM, sds(4, cx, cy, 128),
                [vm(4, cy, 128), vm(4, cy, 128), vm(4, cx, 8, 128), vm(4, cx, 8, 128),
                 vm(4, cx, 128), vm(4, cx, 128), dma(4)],
                2 << 20,
                input_output_aliases={0: 0},
            ),
        )

    return kernels


def shards(
    adjoint, velocity, diffusivity, concentration, heights, receptors, face_src, face_dst, face_coef
):
    nx, ny = lax.axis_size("gx"), lax.axis_size("gy")
    cx, cy, levels = adjoint.shape[1:]
    owners, cap = face_src.shape[2:]
    kernels = make_kernels(nx, ny, cx, cy, owners, cap)
    first, second, third, fourth, fifth, sixth, seventh = kernels(receptors.shape[2])

    def swap(partner):
        return [
            (x * ny + y, px * ny + py)
            for x in range(nx) for y in range(ny) for px, py in (partner(x, y),)
        ]

    def odd(i):
        return i - 1 if i % 2 == 0 else i + 1

    x_even = swap(lambda x, y: (x ^ 1, y))
    x_odd = swap(lambda x, y: (odd(x), y) if 0 < x < nx - 1 else (x, y ^ 1))
    y_even = swap(lambda x, y: (x, y ^ 1))
    y_odd = swap(lambda x, y: (x, odd(y)) if 0 < y < ny - 1 else (x ^ 1, y))

    def exchange(*edges):
        swaps = (x_even, x_odd, y_even, y_odd)
        return [lax.ppermute(e, ("gx", "gy"), pairs) for e, pairs in zip(edges, swaps)]

    src = face_src.reshape(owners, cap)
    dst = face_dst.reshape(owners, cap)
    weight = face_coef.reshape(owners * cap, levels)
    line = receptors.reshape(1, -1)
    flat = adjoint.reshape(4, cx * cy, levels)

    def pinned(*arrays):
        return [pltpu.with_memory_space_constraint(x, pltpu.HBM) for x in arrays]

    conc, counts, *own = first(*pinned(flat, velocity, diffusivity, concentration, line))
    halos = exchange(*own)
    now, soon, hot, weight, *fluid = second(
        conc, counts, *pinned(velocity, diffusivity, heights, src, weight)
    )
    blocks = third(*[halos[n] for n in [0, 1, 3, 2]], *own, *fluid, now, soon, hot, weight)
    arrived = lax.all_to_all(blocks, "gx", split_axis=0, concat_axis=0, tiled=True)
    last, coefs, hot, *rest = fourth(
        *pinned(adjoint, velocity, diffusivity, concentration, line, heights, dst), *[halos[n] for n in [0, 1, 3, 2]]
    )
    edges, sides = rest[:4], rest[4:]
    wall, *edges = fifth(arrived, hot, *edges)
    halos = exchange(*edges)
    out, *strips = sixth(*pinned(last), coefs, wall, arrived, hot)
    return seventh(*pinned(out), *strips, *[halos[n] for n in [0, 1, 3, 2]], *sides)


def solution(mesh):
    placed = (
        P(None, "gx", "gy", None),
        P(None, "gx", "gy", None),
        P("gx", "gy", None),
        P("gx", "gy", None),
        P("gx", "gy"),
        P("gx", "gy", None),
        P("gx", "gy", None, None),
        P("gx", "gy", None, None),
        P("gx", "gy", None, None, None),
    )
    return jax.shard_map(
        shards, mesh=mesh, in_specs=placed, out_specs=P(None, "gx", "gy", None), check_vma=False
    )
```

```python
import jax
import jax.numpy as jnp
from jax import lax
from jax.experimental import pallas as pl
from jax.experimental.pallas import tpu as pltpu
from jax.sharding import PartitionSpec as P

F32 = jnp.float32
BF16 = jnp.bfloat16
PADY = 8
VMEM = pl.BlockSpec(memory_space=pltpu.VMEM)
HBM = pl.BlockSpec(memory_space=pltpu.HBM)


def split3(x):
    hi = x.astype(BF16)
    rest = x - hi.astype(F32)
    mid = rest.astype(BF16)
    low = (rest - mid.astype(F32)).astype(BF16)
    return jnp.concatenate([hi, mid, low], axis=1)


def join3(x):
    return x[:, :128] + x[:, 128:256] + x[:, 256:384]


def row_values(table):
    n = table.shape[1]
    eye = lax.broadcasted_iota(jnp.int32, (n, n), 0) == lax.broadcasted_iota(jnp.int32, (n, n), 1)
    high = table >> 4
    low = table & 15
    ones = jnp.ones((n, 128), BF16)
    total = None
    for part in (high * 16, low):
        part = part.astype(F32)
        rows = [
            jnp.where(eye, jnp.broadcast_to(part[d : d + 1], (n, n)), 0.0)
            for d in range(table.shape[0])
        ]
        spread = jnp.concatenate(rows, axis=0).astype(BF16)
        value = jnp.dot(spread, ones, preferred_element_type=F32)
        total = value if total is None else total + value
    return total


def select_cols(table, cols):
    d_count, n = table.shape
    slots = d_count * n
    tile = (
        lax.broadcasted_iota(jnp.int32, (n, slots), 1) % n
        == lax.broadcasted_iota(jnp.int32, (n, slots), 0)
    ).astype(F32).astype(BF16)
    mine = (
        lax.broadcasted_iota(jnp.int32, (d_count, slots), 1) // n
        == lax.broadcasted_iota(jnp.int32, (d_count, slots), 0)
    )
    high = ((table >> 4) * 16).astype(F32).astype(BF16)
    low = (table & 15).astype(F32).astype(BF16)
    value = jnp.dot(high, tile, preferred_element_type=F32) + jnp.dot(
        low, tile, preferred_element_type=F32
    )
    line = jnp.sum(jnp.where(mine, value, 0.0), axis=0, keepdims=True).astype(jnp.int32)
    col = lax.broadcasted_iota(jnp.int32, (cols, slots), 0)
    return (col == line).astype(F32).astype(BF16)


def receptor_counts(line, cols):
    entries = line.shape[1]
    col = lax.broadcasted_iota(jnp.int32, (cols, entries), 0)
    level = lax.broadcasted_iota(jnp.int32, (128, entries), 0)
    hot_col = (col == (line >> 7)).astype(F32).astype(BF16)
    hot_level = (level == (line & 127)).astype(F32).astype(BF16)
    return lax.dot_general(
        hot_col, hot_level, (((1,), (1,)), ((), ())), preferred_element_type=F32
    )


def make_kernels(nx, ny, cx, cy, owners, cap):
    cols = cx * cy
    slots = owners * cap
    px, py = cx + 2, cy + 2 * PADY
    inside = (pl.ds(1, cx), pl.ds(PADY, cy))

    def edges_at():
        par_x = lax.rem(lax.axis_index("gx"), 2)
        par_y = lax.rem(lax.axis_index("gy"), 2)
        return (
            (cx - 1) * (1 - par_x), (cx - 1) * par_x,
            (cy - 1) * (1 - par_y), (cy - 1) * par_y,
        )

    def start_all(copies):
        for copy in copies:
            copy.start()

    def wait_all(copies):
        for copy in copies:
            copy.wait()

    def clear_halo(pad_ref, planes):
        zero = jnp.zeros((px, PADY, 128), F32)
        row = jnp.zeros((cy, 128), F32)
        for k in planes:
            pad_ref[k, :, 0:PADY, :] = zero
            pad_ref[k, :, PADY + cy : py, :] = zero
            pad_ref[k, 0, PADY : PADY + cy, :] = row
            pad_ref[k, cx + 1, PADY : PADY + cy, :] = row

    def take_halo(pad_ref, plane, n, xe_ref, xo_ref, ye_ref, yo_ref, with_x, with_y):
        me_x, me_y = lax.axis_index("gx"), lax.axis_index("gy")
        par_x, par_y = lax.rem(me_x, 2), lax.rem(me_y, 2)
        if with_x:
            e, o = xe_ref[n], xo_ref[n]
            before = jnp.where(par_x == 0, o, e)
            after = jnp.where(par_x == 0, e, o)
            pad_ref[plane, 0, PADY : PADY + cy, :] = jnp.where(me_x == 0, 0.0, before)
            pad_ref[plane, cx + 1, PADY : PADY + cy, :] = jnp.where(me_x == nx - 1, 0.0, after)
        if with_y:
            e, o = ye_ref[n], yo_ref[n]
            before = jnp.where(me_y == 0, 0.0, jnp.where(par_y == 0, o, e))
            after = jnp.where(me_y == ny - 1, 0.0, jnp.where(par_y == 0, e, o))
            for i in range(cx):
                pad_ref[plane, i + 1, PADY - 1 : PADY, :] = before[i : i + 1]
                pad_ref[plane, i + 1, PADY + cy : PADY + cy + 1, :] = after[i : i + 1]

    def fill_pads(pad_ref, vel_ref, dif_ref, con_ref=None):
        pad_ref[0, 1 : cx + 1, PADY : PADY + cy, :] = vel_ref[0].astype(F32)
        pad_ref[1, 1 : cx + 1, PADY : PADY + cy, :] = vel_ref[1].astype(F32)
        pad_ref[2, 1 : cx + 1, PADY : PADY + cy, :] = dif_ref[...].astype(F32)
        if con_ref is not None:
            pad_ref[3, 1 : cx + 1, PADY : PADY + cy, :] = con_ref[...].astype(F32)

    def cell_coefficients(i, jv, uz, pad_ref, fluid_ref):
        lane = lax.broadcasted_iota(jnp.int32, (8, 128), 1)
        top = lane == 127
        bottom = lane == 0

        def up(x):
            return jnp.where(top, 0.0, pltpu.roll(x, 127, axis=1))

        def down(x):
            return jnp.where(bottom, 0.0, pltpu.roll(x, 1, axis=1))

        j = PADY + 8 * jv
        at = pl.ds(i * cy + 8 * jv, 8)
        fluid = (lane.astype(F32) >= fluid_ref[at, :]).astype(F32)
        e = 0.05 * fluid
        k0 = pad_ref[2, i + 1, j : j + 8, :]
        ends = None
        out = [None]
        for plane, sign, a, b in (
            (0, 1.0, i + 2, j), (0, -1.0, i, j), (1, 1.0, i + 1, j + 1), (1, -1.0, i + 1, j - 1),
        ):
            kn = k0 + pad_ref[2, a, b : b + 8, :]
            un = pad_ref[plane, a, b : b + 8, :]
            out.append(e * (kn + un if sign > 0 else kn - un))
            ends = kn if ends is None else ends + kn
        kn = k0 + up(k0)
        ends = ends + kn
        out.append(jnp.where(top, 0.0, e * (kn + up(uz))))
        kn = k0 + down(k0)
        ends = ends + kn
        out.append(jnp.where(bottom, 0.0, e * (kn - down(uz))))
        out[0] = fluid - e * ends
        return out, e

    def cell_gradients(i, jv, e, pad_ref):
        lane = lax.broadcasted_iota(jnp.int32, (8, 128), 1)
        j = PADY + 8 * jv
        c0 = pad_ref[3, i + 1, j : j + 8, :]
        above = jnp.where(lane == 127, 0.0, pltpu.roll(c0, 127, axis=1))
        below = jnp.where(lane == 0, 0.0, pltpu.roll(c0, 1, axis=1))
        return [
            e * (pad_ref[3, i + 2, j : j + 8, :] - pad_ref[3, i, j : j + 8, :]),
            e * (pad_ref[3, i + 1, j + 1 : j + 9, :] - pad_ref[3, i + 1, j - 1 : j + 7, :]),
            e * (above - below),
        ]

    def cells():
        return [(i, jv) for i in range(cx) for jv in range(cy // 8)]

    def vertical(vel_ref, i, jv):
        pair = vel_ref[2, i, 16 * (jv // 2) : 16 * (jv // 2) + 16, :].astype(F32)
        return pair[8 * (jv % 2) : 8 * (jv % 2) + 8]

    def cell_step(i, jv, c, state_ref, k):
        j = PADY + 8 * jv
        f = state_ref[k, i + 1, j : j + 8, :]
        value = c[0] * f
        value = value + c[1] * state_ref[k, i + 2, j : j + 8, :]
        value = value + c[2] * state_ref[k, i, j : j + 8, :]
        value = value + c[3] * state_ref[k, i + 1, j + 1 : j + 9, :]
        value = value + c[4] * state_ref[k, i + 1, j - 1 : j + 7, :]
        value = value + c[5] * pltpu.roll(f, 127, axis=1)
        value = value + c[6] * pltpu.roll(f, 1, axis=1)
        return value

    def edge_row(ref, k, row):
        return ref[k, pl.ds(pl.multiple_of(row * cy, 8), cy), :]

    def edge_col(ref, k, col):
        return ref[k, pl.ds(col, cx, stride=cy), :]

    def first(
        adj_hbm, vel_hbm, dif_hbm, con_hbm, rec_hbm,
        conc_ref, count_ref, xe_ref, xo_ref, ye_ref, yo_ref,
        adj_ref, vel_ref, dif_ref, con_ref, rec_ref, side_ref, sem,
    ):
        copies = [
            pltpu.make_async_copy(rec_hbm, rec_ref, sem.at[0]),
            pltpu.make_async_copy(vel_hbm.at[pl.ds(0, 2)], vel_ref, sem.at[1]),
            pltpu.make_async_copy(dif_hbm, dif_ref, sem.at[2]),
            pltpu.make_async_copy(con_hbm, con_ref, sem.at[3]),
            pltpu.make_async_copy(adj_hbm, adj_ref, sem.at[4]),
        ]
        start_all(copies)
        row_e, row_o, col_e, col_o = edges_at()
        copies[0].wait()
        counts = receptor_counts(rec_ref[...], cols)
        count_ref[...] = counts
        wait_all(copies[1:4])
        side_ref[0] = vel_ref[1].astype(F32).reshape(cols, 128)
        side_ref[1] = dif_ref[...].astype(F32).reshape(cols, 128)
        side_ref[2] = con_ref[...].astype(F32).reshape(cols, 128)
        for row, out in ((row_e, xe_ref), (row_o, xo_ref)):
            out[4] = vel_ref[0, row].astype(F32)
            out[5] = dif_ref[row].astype(F32)
            out[6] = con_ref[row].astype(F32)
        for col, out in ((col_e, ye_ref), (col_o, yo_ref)):
            for k in range(3):
                out[4 + k] = edge_col(side_ref, k, col)
        copies[4].wait()
        conc = adj_ref[3] + counts
        adj_ref[3] = conc
        conc_ref[...] = conc
        for k in range(4):
            xe_ref[k] = edge_row(adj_ref, k, row_e)
            xo_ref[k] = edge_row(adj_ref, k, row_o)
            ye_ref[k] = edge_col(adj_ref, k, col_e)
            yo_ref[k] = edge_col(adj_ref, k, col_o)

    def second(
        conc_ref, count_ref, vel_hbm, dif_hbm, height_hbm, src_hbm, weight_hbm,
        now_ref, soon_ref, hot_ref, weight_ref, exe_ref, exo_ref, eye_ref, eyo_ref,
        state_ref, vel_ref, dif_ref, height_ref, src_ref,
        pad_ref, fluid_ref, next_ref, sem,
    ):
        copies = [
            pltpu.make_async_copy(src_hbm, src_ref, sem.at[0]),
            pltpu.make_async_copy(height_hbm, height_ref, sem.at[1]),
            pltpu.make_async_copy(dif_hbm, dif_ref, sem.at[2]),
            pltpu.make_async_copy(vel_hbm, vel_ref, sem.at[3]),
            pltpu.make_async_copy(weight_hbm, weight_ref, sem.at[4]),
        ]
        start_all(copies)
        row_e, row_o, col_e, col_o = edges_at()
        clear_halo(pad_ref, range(3))
        clear_halo(state_ref, range(1))
        copies[0].wait()
        index = row_values(src_ref[...]).astype(jnp.int32)
        copies[1].wait()
        fluid_ref[...] = row_values(height_ref[...])
        state_ref[0, 1 : cx + 1, PADY : PADY + cy, :] = conc_ref[...].reshape(cx, cy, 128)
        wait_all(copies[2:4])
        fill_pads(pad_ref, vel_ref, dif_ref)
        for i, jv in cells():
            at = pl.ds(i * cy + 8 * jv, 8)
            c, e = cell_coefficients(i, jv, vertical(vel_ref, i, jv), pad_ref, fluid_ref)
            fluid_ref[at, :] = e
            next_ref[at, :] = cell_step(i, jv, c, state_ref, 0) + count_ref[at, :]
        lane = lax.broadcasted_iota(jnp.int32, index.shape, 1)
        i, j = index // cy, index % cy
        near = jnp.logical_or(
            jnp.logical_or(
                jnp.logical_and(i == row_e, j == lane),
                jnp.logical_and(i == row_o, j + cy == lane),
            ),
            jnp.logical_or(
                jnp.logical_and(j == col_e, i + 2 * cy == lane),
                jnp.logical_and(j == col_o, i + 2 * cy + cx == lane),
            ),
        )
        hot_ref[...] = jnp.where(jnp.logical_and(near, index >= 0), 1.0, 0.0).astype(BF16)
        hot = [(index == lane + t).astype(F32).astype(BF16) for t in range(0, cols, 128)]
        hot = jnp.concatenate(hot, axis=1)
        copies[4].wait()
        weight = weight_ref[...]
        conc = conc_ref[...]
        both = jnp.concatenate([split3(conc), split3(next_ref[...])], axis=1)
        picked = jnp.dot(hot, both, preferred_element_type=F32)
        now_ref[...] = weight * join3(picked[:, :384])
        soon_ref[...] = weight * join3(picked[:, 384:])
        exe_ref[...] = fluid_ref[pl.ds(pl.multiple_of(row_e * cy, 8), cy), :]
        exo_ref[...] = fluid_ref[pl.ds(pl.multiple_of(row_o * cy, 8), cy), :]
        eye_ref[...] = fluid_ref[pl.ds(col_e, cx, stride=cy), :]
        eyo_ref[...] = fluid_ref[pl.ds(col_o, cx, stride=cy), :]

    def edge_signs():
        me_x, me_y = lax.axis_index("gx"), lax.axis_index("gy")
        sx = (1 - 2 * lax.rem(me_x, 2)).astype(F32)
        sy = (1 - 2 * lax.rem(me_y, 2)).astype(F32)
        wrap_x = jnp.logical_or(me_x == 0, me_x == nx - 1)
        wrap_y = jnp.logical_or(me_y == 0, me_y == ny - 1)
        return sx, sy, wrap_x, wrap_y

    def edge_terms(own, halo, e, sign, wrap):
        e = e[...]
        if wrap is not None:
            e = jnp.where(wrap, 0.0, e)
        there = halo[5]
        return e * ((own[5] + there + sign * halo[4]) * halo[3] - there * own[3])

    def third(
        hxe, hxo, hyo, hye, oxe, oxo, oye, oyo, exe, exo, eye, eyo,
        now_ref, soon_ref, hot_ref, weight_ref, blocks_ref,
    ):
        sx, sy, wrap_x, wrap_y = edge_signs()
        edges = [
            edge_terms(oxe, hxe, exe, sx, None),
            edge_terms(oxo, hxo, exo, -sx, wrap_x),
            edge_terms(oye, hye, eye, sy, None),
            edge_terms(oyo, hyo, eyo, -sy, wrap_y),
        ]
        used = 2 * (cx + cy)
        edges = jnp.concatenate(edges + [jnp.zeros((128 - used, 128), F32)], axis=0)
        more = join3(jnp.dot(hot_ref[...], split3(edges), preferred_element_type=F32))
        blocks_ref[:, 0:cap, :] = now_ref[...].reshape(owners, cap, 128)
        soon = soon_ref[...] + weight_ref[...] * more
        blocks_ref[:, cap : 2 * cap, :] = soon.reshape(owners, cap, 128)

    def fourth(
        adj_hbm, vel_hbm, dif_hbm, con_hbm, rec_hbm, height_hbm, dst_hbm, hxe, hxo, hyo, hye,
        last_hbm, coef_out, hot_ref, xe_ref, xo_ref, ye_ref, yo_ref,
        cxe_ref, cxo_ref, cye_ref, cyo_ref,
        state_ref, vel_ref, dif_ref, con_ref, rec_ref, height_ref, dst_ref,
        pad_ref, fluid_ref, count_ref, coef_ref, next_ref, flat_ref, last_ref, sem,
    ):
        copies = [
            pltpu.make_async_copy(height_hbm, height_ref, sem.at[0]),
            pltpu.make_async_copy(vel_hbm, vel_ref, sem.at[1]),
            pltpu.make_async_copy(dif_hbm, dif_ref, sem.at[2]),
            pltpu.make_async_copy(con_hbm, con_ref, sem.at[3]),
            pltpu.make_async_copy(dst_hbm, dst_ref, sem.at[4]),
            pltpu.make_async_copy(rec_hbm, rec_ref, sem.at[5]),
            pltpu.make_async_copy(adj_hbm, state_ref.at[:, inside[0], inside[1], :], sem.at[6]),
        ]
        start_all(copies)
        row_e, row_o, col_e, col_o = edges_at()
        clear_halo(next_ref, range(4))
        halo = (hxe, hxo, hye, hyo)
        take_halo(pad_ref, 0, 4, *halo, True, False)
        take_halo(pad_ref, 1, 4, *halo, False, True)
        take_halo(pad_ref, 2, 5, *halo, True, True)
        take_halo(pad_ref, 3, 6, *halo, True, True)
        for k in range(4):
            take_halo(state_ref, k, k, *halo, True, True)
        copies[0].wait()
        fluid_ref[...] = row_values(height_ref[...])
        wait_all(copies[1:4])
        fill_pads(pad_ref, vel_ref, dif_ref, con_ref)
        wait_all(copies[4:7])
        hot_ref[...] = select_cols(dst_ref[...], cols)
        count_ref[...] = receptor_counts(rec_ref[...], cols)
        state_ref[3, 1 : cx + 1, PADY : PADY + cy, :] += count_ref[...].reshape(cx, cy, 128)
        for i, jv in cells():
            at = pl.ds(i * cy + 8 * jv, 8)
            j = PADY + 8 * jv
            c, e = cell_coefficients(i, jv, vertical(vel_ref, i, jv), pad_ref, fluid_ref)
            c = c + cell_gradients(i, jv, e, pad_ref)
            for n in range(10):
                if n < 7:
                    coef_out[n, at, :] = c[n]
                coef_ref[n, at, :] = c[n]
            conc = state_ref[3, i + 1, j : j + 8, :]
            for k in range(4):
                value = cell_step(i, jv, c, state_ref, k)
                value = value + count_ref[at, :] if k == 3 else value - c[7 + k] * conc
                next_ref[k, i + 1, j : j + 8, :] = value
                flat_ref[k, at, :] = value
        for k in range(4):
            xe_ref[k] = edge_row(flat_ref, k, row_e)
            xo_ref[k] = edge_row(flat_ref, k, row_o)
            ye_ref[k] = edge_col(flat_ref, k, col_e)
            yo_ref[k] = edge_col(flat_ref, k, col_o)
        for i, jv in cells():
            at = pl.ds(i * cy + 8 * jv, 8)
            j = PADY + 8 * jv
            c = [coef_ref[n, at, :] for n in range(10)]
            conc = next_ref[3, i + 1, j : j + 8, :]
            for k in range(4):
                value = cell_step(i, jv, c, next_ref, k)
                if k < 3:
                    value = value - c[7 + k] * conc
                last_ref[k, i, 8 * jv : 8 * jv + 8, :] = value
        out = pltpu.make_async_copy(last_ref, last_hbm, sem.at[7])
        out.start()
        par_x = lax.rem(lax.axis_index("gx"), 2)
        par_y = lax.rem(lax.axis_index("gy"), 2)
        cxe_ref[...] = coef_ref[1 + par_x, pl.ds(pl.multiple_of(row_e * cy, 8), cy), :]
        cxo_ref[...] = coef_ref[2 - par_x, pl.ds(pl.multiple_of(row_o * cy, 8), cy), :]
        cye_ref[...] = edge_col(coef_ref, 3 + par_y, col_e)
        cyo_ref[...] = edge_col(coef_ref, 4 - par_y, col_o)
        out.wait()

    def fifth(
        arrived_ref, hot_ref, xe_in, xo_in, ye_in, yo_in,
        wall_ref, xe_ref, xo_ref, ye_ref, yo_ref,
    ):
        row_e, row_o, col_e, col_o = edges_at()
        blocks = split3(arrived_ref[:, 0:cap, :].reshape(slots, 128))
        wall_ref[0] = join3(jnp.dot(hot_ref[...], blocks, preferred_element_type=F32))
        xe_ref[...] = xe_in[...]
        xo_ref[...] = xo_in[...]
        ye_ref[...] = ye_in[...]
        yo_ref[...] = yo_in[...]
        xe_ref[2] += edge_row(wall_ref, 0, row_e)
        xo_ref[2] += edge_row(wall_ref, 0, row_o)
        ye_ref[2] += edge_col(wall_ref, 0, col_e)
        yo_ref[2] += edge_col(wall_ref, 0, col_o)

    def sixth(
        last_hbm, coef_ref, wall_ref, arrived_ref, hot_ref,
        out_hbm, sxe_ref, sxo_ref, sye_ref, syo_ref,
        pad_ref, final_ref, add_ref, sem,
    ):
        row_e, row_o, col_e, col_o = edges_at()
        tile_e = pl.ds(pl.multiple_of(col_e // 8 * 8, 8), 8)
        tile_o = pl.ds(pl.multiple_of(col_o // 8 * 8, 8), 8)
        copies = [
            pltpu.make_async_copy(last_hbm.at[2], final_ref, sem.at[0]),
            pltpu.make_async_copy(last_hbm.at[:, row_e], sxe_ref, sem.at[2]),
            pltpu.make_async_copy(last_hbm.at[:, row_o], sxo_ref, sem.at[3]),
            pltpu.make_async_copy(last_hbm.at[:, :, tile_e, :], sye_ref, sem.at[4]),
            pltpu.make_async_copy(last_hbm.at[:, :, tile_o, :], syo_ref, sem.at[5]),
        ]
        start_all(copies)
        blocks = split3(arrived_ref[:, cap : 2 * cap, :].reshape(slots, 128))
        add_ref[...] = join3(jnp.dot(hot_ref[...], blocks, preferred_element_type=F32))
        clear_halo(pad_ref, (0,))
        pad_ref[0, 1 : cx + 1, PADY : PADY + cy, :] = wall_ref[0].reshape(cx, cy, 128)
        wait_all(copies)
        outs = []
        for i, jv in cells():
            at = pl.ds(i * cy + 8 * jv, 8)
            c = [coef_ref[n, at, :] for n in range(7)]
            value = final_ref[i, 8 * jv : 8 * jv + 8, :] + add_ref[at, :]
            final_ref[i, 8 * jv : 8 * jv + 8, :] = value + cell_step(i, jv, c, pad_ref, 0)
            if (i + 1) % (cx // 4) == 0 and jv == cy // 8 - 1:
                rows = pl.ds(i + 1 - cx // 4, cx // 4)
                done = len(outs)
                outs.append(
                    pltpu.make_async_copy(
                        final_ref.at[rows], out_hbm.at[2, rows], sem.at[6 + done]
                    )
                )
                outs[done].start()
        sxe_ref[2] = final_ref[row_e]
        sxo_ref[2] = final_ref[row_o]
        sye_ref[2] = final_ref[:, tile_e, :]
        syo_ref[2] = final_ref[:, tile_o, :]
        wait_all(outs)

    def seventh(
        last_hbm, sxe, sxo, sye, syo, hxe, hxo, hyo, hye, cxe, cxo, cye, cyo,
        out_hbm, txe, txo, tye, tyo, dye, dyo, sem,
    ):
        row_e, row_o, col_e, col_o = edges_at()
        _, _, wrap_x, wrap_y = edge_signs()
        near_e, near_o = cye[...], jnp.where(wrap_y, 0.0, cyo[...])
        here = lax.broadcasted_iota(jnp.int32, (8, 128), 0)
        tile_e = col_e // 8 * 8
        tile_o = col_o // 8 * 8
        for k in range(4):
            dye[k] = near_e * hye[k]
            dyo[k] = near_o * hyo[k]
            for i in range(1, cx - 1):
                add_e = jnp.broadcast_to(dye[k, i : i + 1, :], (8, 128))
                add_o = jnp.broadcast_to(dyo[k, i : i + 1, :], (8, 128))
                tye[k, i] = sye[k, i] + jnp.where(here == col_e - tile_e, add_e, 0.0)
                tyo[k, i] = syo[k, i] + jnp.where(here == col_o - tile_o, add_o, 0.0)
        copies = [
            pltpu.make_async_copy(
                strip.at[:, pl.ds(1, cx - 2)],
                out_hbm.at[:, pl.ds(1, cx - 2), pl.ds(pl.multiple_of(tile, 8), 8), :],
                sem.at[n],
            )
            for n, (strip, tile) in enumerate(((tye, tile_e), (tyo, tile_o)))
        ]
        start_all(copies)
        near_e, near_o = cxe[...], jnp.where(wrap_x, 0.0, cxo[...])
        for k in range(4):
            txe[k] = sxe[k] + near_e * hxe[k]
            txo[k] = sxo[k] + near_o * hxo[k]
            for row, out in ((row_e, txe), (row_o, txo)):
                for col, dy in ((col_e, dye), (col_o, dyo)):
                    out[k, pl.ds(col, 1), :] += dy[k, pl.ds(row, 1), :]
        more = [
            pltpu.make_async_copy(strip, out_hbm.at[:, row], sem.at[n])
            for n, (strip, row) in enumerate(((txe, row_e), (txo, row_o)), 2)
        ]
        start_all(more)
        wait_all(copies + more)

    def sds(*shape):
        return jax.ShapeDtypeStruct(shape, F32)

    def hbm(*shape):
        return pltpu.HBM(shape, F32)

    def vm(*shape, dtype=F32):
        return pltpu.VMEM(shape, dtype)

    def dma(count):
        return pltpu.SemaphoreType.DMA((count,))

    def call(body, name, ins, outs, shapes, scratch, cost, limit=24, **more):
        return pl.pallas_call(
            body,
            name=name,
            out_shape=shapes,
            in_specs=ins,
            out_specs=outs,
            scratch_shapes=scratch,
            compiler_params=pltpu.CompilerParams(vmem_limit_bytes=limit << 20),
            cost_estimate=pl.CostEstimate(flops=cost, bytes_accessed=cost, transcendentals=0),
            **more,
        )

    int_table = vm(owners, cap, dtype=jnp.int32)
    three = [vm(3, cx, cy, 128, dtype=BF16)] + [vm(cx, cy, 128, dtype=BF16)] * 2
    strips = (sds(4, cy, 128), sds(4, cy, 128), sds(4, cx, 128), sds(4, cx, 128))
    sides = (sds(cy, 128), sds(cy, 128), sds(cx, 128), sds(cx, 128))
    height = vm(cx, cy, dtype=jnp.int32)
    padded = vm(4, px, py, 128)

    def kernels(rcp):
        line = vm(1, rcp, dtype=jnp.int32)
        return (
            call(
                first, "first", [HBM] * 5, (VMEM,) * 6,
                (sds(cols, 128), sds(cols, 128), sds(7, cy, 128), sds(7, cy, 128), sds(7, cx, 128), sds(7, cx, 128)),
                [vm(4, cols, 128), vm(2, cx, cy, 128, dtype=BF16)] + three[1:]
                + [line, vm(3, cols, 128), dma(5)],
                4 << 20,
            ),
            call(
                second, "second", [VMEM] * 2 + [HBM] * 5, (VMEM,) * 8,
                (sds(slots, 128), sds(slots, 128),
                 jax.ShapeDtypeStruct((slots, 128), BF16), sds(slots, 128)) + sides,
                [vm(1, px, py, 128)] + three[:2] + [height, int_table]
                + [vm(3, px, py, 128), vm(cols, 128), vm(cols, 128), dma(5)],
                8 << 20,
            ),
            call(
                third, "third", [VMEM] * 16, VMEM, sds(owners, 2 * cap, 128), [], 2 << 20,
            ),
            call(
                fourth, "fourth", [HBM] * 7 + [VMEM] * 4, (HBM,) + (VMEM,) * 10,
                (hbm(4, cx, cy, 128), sds(7, cols, 128), jax.ShapeDtypeStruct((cols, slots), BF16))
                + strips + sides,
                [padded] + three + [line, height, int_table]
                + [padded, vm(cols, 128), vm(cols, 128), vm(10, cols, 128), padded,
                   vm(4, cols, 128), vm(4, cx, cy, 128), dma(8)],
                10 << 20,
            ),
            call(
                fifth, "fifth", [VMEM] * 6, (VMEM,) * 5, (sds(1, cols, 128),) + strips, [],
                2 << 20,
            ),
            call(
                sixth, "sixth", [HBM] + [VMEM] * 4, (HBM,) + (VMEM,) * 4,
                (hbm(4, cx, cy, 128), sds(4, cy, 128), sds(4, cy, 128),
                 sds(4, cx, 8, 128), sds(4, cx, 8, 128)),
                [vm(1, px, py, 128), vm(cx, cy, 128), vm(cols, 128), dma(10)],
                5 << 20,
                input_output_aliases={0: 0},
            ),
            call(
                seventh, "seventh", [HBM] + [VMEM] * 12, HBM, sds(4, cx, cy, 128),
                [vm(4, cy, 128), vm(4, cy, 128), vm(4, cx, 8, 128), vm(4, cx, 8, 128),
                 vm(4, cx, 128), vm(4, cx, 128), dma(4)],
                2 << 20,
                input_output_aliases={0: 0},
            ),
        )

    return kernels


def shards(
    adjoint, velocity, diffusivity, concentration, heights, receptors, face_src, face_dst, face_coef
):
    nx, ny = lax.axis_size("gx"), lax.axis_size("gy")
    cx, cy, levels = adjoint.shape[1:]
    owners, cap = face_src.shape[2:]
    kernels = make_kernels(nx, ny, cx, cy, owners, cap)
    first, second, third, fourth, fifth, sixth, seventh = kernels(receptors.shape[2])

    def swap(partner):
        return [
            (x * ny + y, px * ny + py)
            for x in range(nx) for y in range(ny) for px, py in (partner(x, y),)
        ]

    def odd(i):
        return i - 1 if i % 2 == 0 else i + 1

    x_even = swap(lambda x, y: (x ^ 1, y))
    x_odd = swap(lambda x, y: (odd(x), y) if 0 < x < nx - 1 else (x, y ^ 1))
    y_even = swap(lambda x, y: (x, y ^ 1))
    y_odd = swap(lambda x, y: (x, odd(y)) if 0 < y < ny - 1 else (x ^ 1, y))

    def exchange(*edges):
        swaps = (x_even, x_odd, y_even, y_odd)
        return [lax.ppermute(e, ("gx", "gy"), pairs) for e, pairs in zip(edges, swaps)]

    src = face_src.reshape(owners, cap)
    dst = face_dst.reshape(owners, cap)
    weight = face_coef.reshape(owners * cap, levels)
    line = receptors.reshape(1, -1)
    flat = adjoint.reshape(4, cx * cy, levels)

    def pinned(*arrays):
        return [pltpu.with_memory_space_constraint(x, pltpu.HBM) for x in arrays]

    conc, counts, *own = first(*pinned(flat, velocity, diffusivity, concentration, line))
    halos = exchange(*own)
    now, soon, hot, weight, *fluid = second(
        conc, counts, *pinned(velocity, diffusivity, heights, src, weight)
    )
    blocks = third(*[halos[n] for n in [0, 1, 3, 2]], *own, *fluid, now, soon, hot, weight)
    arrived = lax.all_to_all(blocks, "gx", split_axis=0, concat_axis=0, tiled=True)
    last, coefs, hot, *rest = fourth(
        *pinned(adjoint, velocity, diffusivity, concentration, line, heights, dst), *[halos[n] for n in [0, 1, 3, 2]]
    )
    edges, sides = rest[:4], rest[4:]
    wall, *edges = fifth(arrived, hot, *edges)
    halos = exchange(*edges)
    out, *strips = sixth(*pinned(last), coefs, wall, arrived, hot)
    return seventh(*pinned(out), *strips, *[halos[n] for n in [0, 1, 3, 2]], *sides)


def solution(mesh):
    placed = (
        P(None, "gx", "gy", None),
        P(None, "gx", "gy", None),
        P("gx", "gy", None),
        P("gx", "gy", None),
        P("gx", "gy"),
        P("gx", "gy", None),
        P("gx", "gy", None, None),
        P("gx", "gy", None, None),
        P("gx", "gy", None, None, None),
    )
    return jax.shard_map(
        shards, mesh=mesh, in_specs=placed, out_specs=P(None, "gx", "gy", None), check_vma=False
    )
```
